32 devices in a mesh: ctx: 8 (over z, x), fsdp: 4 (over y, core).
Axes of the slice: x: 2, y: 2, z: 4, core: 2. Of those that a mesh axis runs over, the one named last changes fastest.
Arguments:
- tokens: bfloat16 [4, 1024, 2048], P('fsdp', 'ctx'), may hold values from -6 to 6
- ln1_gain: float32 [2048], P(('ctx', 'fsdp')), may hold values from 0.5 to 1.5
- ln1_bias: float32 [2048], P(('ctx', 'fsdp')), may hold values from -3 to 3
- w_qkv: float32 [2048, 6144], P(('ctx', 'fsdp')), may hold values from -0.125 to 0.125
- b_qv: float32 [4096], P(('ctx', 'fsdp')), may hold values from -3 to 3
- w_out: float32 [2048, 2048], P(('ctx', 'fsdp')), may hold values from -0.375 to 0.375
- b_out: float32 [2048], P(('ctx', 'fsdp')), may hold values from -3 to 3
- ln2_gain: float32 [2048], P(('ctx', 'fsdp')), may hold values from 0.5 to 1.5
- ln2_bias: float32 [2048], P(('ctx', 'fsdp')), may hold values from -3 to 3
- w_in: float32 [2048, 8192], P(('ctx', 'fsdp')), may hold values from -0.125 to 0.125
- b_in: float32 [8192], P(('ctx', 'fsdp')), may hold values from -3 to 3
- w_down: float32 [8192, 2048], P(('ctx', 'fsdp')), may hold values from -0.09375 to 0.09375
- b_down: float32 [2048], P(('ctx', 'fsdp')), may hold values from -3 to 3
- cotangent: bfloat16 [4, 1024, 2048], P('fsdp', 'ctx'), may hold values from -6 to 6
- block_seg: int32 [4, 8], P('fsdp'), may hold values from 0 to 1, as said below
- block_pos: int32 [4, 8], P('fsdp'), may hold values from 0 to 896, as said below
Outputs:
- output: bfloat16 [4, 1024, 2048], P('fsdp', 'ctx')
- grad_tokens: float32 [4, 1024, 2048], P('fsdp', 'ctx')
- grad_ln1_gain: float32 [2048], P(('ctx', 'fsdp'))
- grad_ln1_bias: float32 [2048], P(('ctx', 'fsdp'))
- grad_w_qkv: float32 [2048, 6144], P(('ctx', 'fsdp'))
- grad_b_qv: float32 [4096], P(('ctx', 'fsdp'))
- grad_w_out: float32 [2048, 2048], P(('ctx', 'fsdp'))
- grad_b_out: float32 [2048], P(('ctx', 'fsdp'))
- grad_ln2_gain: float32 [2048], P(('ctx', 'fsdp'))
- grad_ln2_bias: float32 [2048], P(('ctx', 'fsdp'))
- grad_w_in: float32 [2048, 8192], P(('ctx', 'fsdp'))
- grad_b_in: float32 [8192], P(('ctx', 'fsdp'))
- grad_w_down: float32 [8192, 2048], P(('ctx', 'fsdp'))
- grad_b_down: float32 [2048], P(('ctx', 'fsdp'))
The draws below stay inside these ranges and needn't reach their ends.
Inputs may be any that keep to these rules, and one draw needn't show every extreme that they name: `block_seg`: in each group the stored blocks are the prompt's 512 // 128 blocks (segment 0, offsets 0, 128, 256, ...) and, for each continuation s, its 4 blocks (segment s, offsets 512, 640, ...), each once, in an order that varies; the first stored block is the prompt's first one and the last stored block is the prompt's last one. `block_pos`: offsets that go with block_seg as described there.
All inputs are finite; a program needn't handle non-finite values.
Results may differ from the reference program's by a relative error of at most 0.019.
Values may be sent and summed in bfloat16 or wider, within the bound.
No kernel may reach another device: no remote copies, remote signals or barrier semaphores. Data moves between devices by JAX's collectives and lax.ppermute only.
A program may use at most 384 MiB of HBM per device.

```python
import math
import jax
import jax.numpy as jnp
from jax import lax

D = 2048
H = 16
HD = 128
FF = 8192
BLK = 128
CONT_LEN = 512
GROUP_LEN = 1024
PROMPT_LEN = 512
GROUPS = 4


def block_layout(key):
    block_total = GROUP_LEN // BLK
    prompt_blocks = PROMPT_LEN // BLK
    cont_blocks = CONT_LEN // BLK
    middle = jnp.concatenate([jnp.arange(1, prompt_blocks - 1, dtype=jnp.int32), jnp.arange(prompt_blocks, block_total, dtype=jnp.int32)])

    def one_group(group_id):
        shuffled = jax.random.permutation(jax.random.fold_in(jax.random.fold_in(key, 17), group_id), middle)
        stored_order = jnp.concatenate([jnp.zeros((1,), jnp.int32), shuffled.astype(jnp.int32), jnp.full((1,), prompt_blocks - 1, jnp.int32)])
        in_prompt = stored_order < prompt_blocks
        seg_ids = jnp.where(in_prompt, 0, 1 + (stored_order - prompt_blocks) // cont_blocks)
        offsets = jnp.where(in_prompt, stored_order * BLK, PROMPT_LEN + (stored_order - prompt_blocks) % cont_blocks * BLK)
        return (seg_ids.astype(jnp.int32), offsets.astype(jnp.int32))
    return jax.vmap(one_group)(jnp.arange(GROUPS, dtype=jnp.int32))


def draw_block_seg(key, part):
    return block_layout(key)[0]


def draw_block_pos(key, part):
    return block_layout(key)[1]


def with_spikes(array, rng, source, target, blocks, factor):
    def block_of(axis_at):
        return (jnp.arange(array.shape[axis_at]) // (array.shape[axis_at] // blocks)).reshape((-1,) + (1,) * (array.ndim - 1 - axis_at))

    near = jax.random.permutation(rng, blocks)[block_of(target)]
    other_side = (block_of(target) + blocks // 2) % blocks
    return jnp.where((block_of(source) == near) | (block_of(source) == other_side), factor * array, array)


def block_scale(key, dims, shards, smallest, largest):
    def one(dim, parts):
        draws = jax.random.uniform(jax.random.fold_in(jax.random.fold_in(key, 6), dim), (parts,), jnp.float32, smallest / len(shards), largest / len(shards))
        return jnp.repeat(jnp.exp(draws), dims[dim] // parts).reshape((-1,) + (1,) * (len(dims) - dim - 1))

    gain = one(*shards[0])
    for cut in shards[1:]:
        gain = gain * one(*cut)
    return gain


def bell_draw(stream_key, dims, scale, reach, shards=(), held_as=jnp.bfloat16):
    values = jax.random.normal(stream_key, dims, jnp.float32) * scale
    if len(shards) > 0:
        values = block_scale(stream_key, dims, shards, -0.22, 0.18) * values
    return jnp.clip(values, min=-reach, max=reach).astype(held_as)


def noise_with(rng, extent, width, most, shards, heavy, kind=jnp.bfloat16):
    entries = width * jax.random.normal(rng, extent, jnp.float32)
    if shards:
        entries = entries * block_scale(rng, extent, shards, -0.22, 0.18)
    return jnp.clip(with_spikes(entries, jax.random.fold_in(rng, 3), *heavy), -most, most).astype(kind)


def setup_inputs(seed: int = 0) -> dict:
    splits = jax.random.split(jax.random.key(seed), 17)
    return {
        "tokens": bell_draw(splits[0], (GROUPS, GROUP_LEN, D), 1.0, 6.0, ((0, 4), (1, 8))),
        "ln1_gain": jnp.clip(1.0 + 0.1 * jax.random.normal(splits[1], (D,), jnp.float32), 0.5, 1.5),
        "ln1_bias": bell_draw(splits[2], (D,), 0.2, 3.0, ((0, 32),), jnp.float32),
        "w_qkv": bell_draw(splits[3], (D, 3 * D), D ** -0.5, 0.125, ((0, 32),), jnp.float32),
        "b_qv": bell_draw(splits[4], (2 * D,), 0.2, 3.0, ((0, 32),), jnp.float32),
        "w_out": bell_draw(splits[5], (D, D), (D // 8) ** -0.5, 0.375, ((0, 32),), jnp.float32),
        "b_out": bell_draw(splits[6], (D,), 0.2, 3.0, ((0, 32),), jnp.float32),
        "ln2_gain": jnp.clip(1.0 + 0.1 * jax.random.normal(splits[7], (D,), jnp.float32), 0.5, 1.5),
        "ln2_bias": bell_draw(splits[8], (D,), 0.2, 3.0, ((0, 32),), jnp.float32),
        "w_in": bell_draw(splits[9], (D, FF), D ** -0.5, 0.125, ((0, 32),), jnp.float32),
        "b_in": bell_draw(splits[10], (FF,), 0.2, 3.0, ((0, 32),), jnp.float32),
        "w_down": bell_draw(splits[11], (FF, D), (FF // 2) ** -0.5, 0.09375, ((0, 32),), jnp.float32),
        "b_down": bell_draw(splits[12], (D,), 0.2, 3.0, ((0, 32),), jnp.float32),
        "cotangent": noise_with(splits[13], (GROUPS, GROUP_LEN, D), 1.0, 6.0, ((0, 4), (1, 8)), (1, 2, 8, 2.0)),
        "block_seg": draw_block_seg(jax.random.fold_in(splits[16], 71), 0),
        "block_pos": draw_block_pos(jax.random.fold_in(splits[16], 71), 0),
    }


@jax.custom_vjp
def low(v):
    return lax.optimization_barrier(v.astype(jnp.bfloat16)).astype(jnp.float32)

@jax.custom_vjp
def low_back(v):
    return v

def low_keep(v):
    return (low(v), None)

def low_pass(kept, grad):
    return (grad,)

def back_keep(v):
    return (v, None)

def back_low(kept, grad):
    return (low(grad),)
low.defvjp(low_keep, low_pass)
low_back.defvjp(back_keep, back_low)
EPSILON = 1e-05
NEG_FILL = -1e+30

def norm_rows(values, norm_gain, norm_bias):
    center = values - lax.optimization_barrier(jnp.mean(values, axis=-1, keepdims=True))
    spread = lax.optimization_barrier(jnp.mean(center * center, axis=-1, keepdims=True))
    return center * lax.rsqrt(spread + EPSILON) * norm_gain + norm_bias

def alibi_slopes():
    return jnp.exp2(-8.0 * (jnp.arange(H, dtype=jnp.float32) + 1.0) / H)

def token_meta(block_seg, block_pos):
    offsets = jnp.arange(BLK, dtype=jnp.int32)
    seg_tok = jnp.repeat(block_seg, BLK, axis=1).astype(jnp.int32)
    pos_tok = (block_pos[:, :, None] + offsets[None, None, :]).reshape(block_pos.shape[0], -1).astype(jnp.int32)
    return (seg_tok, pos_tok)

def reference(tokens, ln1_gain, ln1_bias, w_qkv, b_qv, w_out, b_out, ln2_gain, ln2_bias, w_in, b_in, w_down, b_down, cotangent, block_seg, block_pos):
    highest = lax.Precision.HIGHEST
    seg_tok, pos_tok = token_meta(block_seg, block_pos)
    slopes = alibi_slopes()
    scale_qk = 1.0 / math.sqrt(HD)
    rows_block = math.gcd(GROUP_LEN, 512)
    block_count = GROUP_LEN // rows_block

    def attend(query_all, key_all, value_all):
        query_blocks = query_all.reshape(GROUPS * block_count, rows_block, H, HD)
        seg_blocks = seg_tok.reshape(GROUPS * block_count, rows_block)
        pos_blocks = pos_tok.reshape(GROUPS * block_count, rows_block)
        group_ids = (jnp.arange(GROUPS * block_count, dtype=jnp.int32) // block_count).astype(jnp.int32)

        def one_block(block_items):
            query_rows, query_seg, query_pos, group_id = block_items
            key_rows = lax.dynamic_index_in_dim(key_all, group_id, 0, keepdims=False)
            value_rows = lax.dynamic_index_in_dim(value_all, group_id, 0, keepdims=False)
            key_seg = lax.dynamic_index_in_dim(seg_tok, group_id, 0, keepdims=False)
            key_pos = lax.dynamic_index_in_dim(pos_tok, group_id, 0, keepdims=False)
            distance = (query_pos[:, None] - key_pos[None, :]).astype(jnp.float32)
            scores = jnp.einsum('qhd,khd->hqk', query_rows, key_rows, precision=highest) * scale_qk - slopes[:, None, None] * distance[None]
            scores = low_back(scores)
            visible = ((key_seg[None, :] == 0) | (key_seg[None, :] == query_seg[:, None])) & (key_pos[None, :] <= query_pos[:, None])
            scores = jnp.where(visible[None], scores, NEG_FILL)
            row_top = lax.optimization_barrier(jnp.max(scores, axis=-1, keepdims=True))
            expon_rows = jnp.exp(scores - row_top)
            probs_soft = expon_rows / lax.optimization_barrier(jnp.sum(expon_rows, axis=-1, keepdims=True))
            return jnp.einsum('hqk,khd->qhd', low(probs_soft), value_rows, precision=highest)
        return lax.map(jax.checkpoint(one_block), (query_blocks, seg_blocks, pos_blocks, group_ids))

    def forward(input_all, gain_first, bias_first, qkv_matrix, qkv_bias, out_matrix, out_bias, gain_second, bias_second, in_matrix, in_bias, down_matrix, down_bias):
        gain_first = low(gain_first)
        bias_first = low(bias_first)
        qkv_matrix = low(qkv_matrix)
        qkv_bias = low(qkv_bias)
        out_matrix = low(out_matrix)
        out_bias = low(out_bias)
        gain_second = low(gain_second)
        bias_second = low(bias_second)
        in_matrix = low(in_matrix)
        in_bias = low(in_bias)
        down_matrix = low(down_matrix)
        down_bias = low(down_bias)
        normed = low(norm_rows(input_all, gain_first, bias_first))
        mixed_rows = jnp.einsum('gtd,de->gte', normed, qkv_matrix, precision=highest)
        query_all = low(low_back(mixed_rows[..., :D] + qkv_bias[:D]))
        key_all = low(low_back(mixed_rows[..., D:2 * D]))
        value_all = low(low_back(mixed_rows[..., 2 * D:] + qkv_bias[D:]))
        shape_heads = (GROUPS, GROUP_LEN, H, HD)
        attended = attend(query_all.reshape(shape_heads), key_all.reshape(shape_heads), value_all.reshape(shape_heads))
        attended = low(low_back(attended.reshape(GROUPS, GROUP_LEN, D)))
        branch = low_back(jnp.einsum('gtd,de->gte', attended, out_matrix, precision=highest) + out_bias)
        residual = input_all + branch
        second = low(norm_rows(residual, gain_second, bias_second))
        pre_act = low_back(jnp.einsum('gtd,df->gtf', second, in_matrix, precision=highest) + in_bias)
        activated = low(jax.nn.gelu(pre_act, approximate=True))
        ffn_out = low_back(jnp.einsum('gtf,fd->gtd', activated, down_matrix, precision=highest) + down_bias)
        return residual + ffn_out
    result, pullback = jax.vjp(forward, tokens.astype(jnp.float32), ln1_gain, ln1_bias, w_qkv, b_qv, w_out, b_out, ln2_gain, ln2_bias, w_in, b_in, w_down, b_down)
    grads = pullback(cotangent.astype(jnp.float32))
    return (result.astype(jnp.bfloat16), grads[0], grads[1], grads[2], grads[3], grads[4], grads[5], grads[6], grads[7], grads[8], grads[9], grads[10], grads[11], grads[12])
```

```python
import math

import jax
import jax.numpy as jnp
from jax import lax
from jax.sharding import Mesh
from jax.sharding import PartitionSpec as P

HD = 128
BLK = 128
EPSILON = 1e-05
NEG_FILL = -1e30

EVERY = ("tp", "sp", "fs")
TOKENS = ("sp", "fs")
SNAKE = (0, 2, 4, 6, 7, 5, 3, 1)


def half(values):
    return values.astype(jnp.bfloat16)


def full(values):
    return values.astype(jnp.float32)


def dot(left, right, left_dim, right_dim, out=jnp.float32):
    return lax.dot_general(
        left, right, (((left_dim,), (right_dim,)), ((), ())), preferred_element_type=jnp.float32
    ).astype(out)


def normalize(values):
    center = values - jnp.mean(values, axis=-1, keepdims=True)
    spread = jnp.mean(center * center, axis=-1, keepdims=True)
    scale = lax.rsqrt(spread + EPSILON)
    return center * scale, scale


def normalize_back(normed, scale, grad):
    return scale * (
        grad
        - jnp.mean(grad, axis=-1, keepdims=True)
        - normed * jnp.mean(grad * normed, axis=-1, keepdims=True)
    )


class Ring:
    def __init__(self, size):
        self.size = size
        order = SNAKE if size == len(SNAKE) else tuple(range(size))
        place = [order.index(i) for i in range(size)]
        self.order = order
        self.up = [(order[i], order[(i + 1) % size]) for i in range(size)]
        self.down = [(b, a) for a, b in self.up]
        self.place = jnp.asarray(place, jnp.int32)[lax.axis_index("tp")]

    def index(self, shift):
        return jnp.asarray(self.order, jnp.int32)[(self.place + shift) % self.size]

    def send_up(self, values):
        return lax.ppermute(values, "tp", self.up)

    def send_down(self, values):
        return lax.ppermute(values, "tp", self.down)

    def gather(self, rows):
        n = rows.shape[0]
        out = jnp.zeros((self.size * n,) + rows.shape[1:], rows.dtype)

        def put(out, chunk, shift, begin=0):
            return lax.dynamic_update_slice_in_dim(out, chunk, self.index(shift) * n + begin, 0)

        out = put(out, rows, 0)
        from_below = from_above = rows
        for hop in range(1, (self.size + 1) // 2):
            from_below, from_above = self.send_up(from_below), self.send_down(from_above)
            out = put(out, from_below, -hop)
            out = put(out, from_above, hop)
        if self.size % 2 == 0:
            low = self.send_up(from_below[: n // 2])
            high = self.send_down(from_above[n // 2 :])
            out = put(out, low, self.size // 2)
            out = put(out, high, self.size // 2, n // 2)
        return out

    def reduce_scatter(self, partial):
        n = partial.shape[0] // self.size
        middle = self.size // 2

        def own(shift):
            return lax.dynamic_slice_in_dim(partial, self.index(shift) * n, n)

        far = own(middle)
        low, high = self.send_up(far[: n // 2]), self.send_down(far[n // 2 :])
        part = own(middle - 1)
        upward = jnp.concatenate([half(full(part[: n // 2]) + full(low)), part[n // 2 :]])
        part = own(1 - middle)
        downward = jnp.concatenate([part[: n // 2], half(full(part[n // 2 :]) + full(high))])
        for hop in range(middle - 2, -1, -1):
            upward, downward = self.send_up(upward), self.send_down(downward)
            if hop:
                upward = half(full(upward) + full(own(hop)))
                downward = half(full(downward) + full(own(-hop)))
        return full(own(0)) + full(upward) + full(downward)


def columns_in(rows, groups, tp):
    n, width = rows.shape
    part = width // groups // tp
    rows = lax.all_to_all(
        rows.reshape(n, groups, tp, part), "tp", split_axis=2, concat_axis=0, tiled=False
    )
    rows = lax.all_gather(rows.reshape(tp, n, groups * part), TOKENS, axis=1, tiled=True)
    return rows.reshape(-1, groups * part)


def columns_out(grad, groups, tp):
    part = grad.shape[1] // groups
    grad = grad.reshape(tp, -1, groups * part)
    grad = lax.psum_scatter(half(grad), TOKENS, scatter_dimension=1, tiled=True)
    n = grad.shape[1]
    grad = lax.all_to_all(
        grad.reshape(tp, n, groups, part), "tp", split_axis=0, concat_axis=2, tiled=False
    )
    return full(grad.reshape(n, groups * tp * part))


def on_device(
    tokens,
    ln1_gain,
    ln1_bias,
    w_qkv,
    b_qv,
    w_out,
    b_out,
    ln2_gain,
    ln2_bias,
    w_in,
    b_in,
    w_down,
    b_down,
    cotangent,
    block_seg,
    block_pos,
):
    tp = lax.axis_size("tp")
    sp = lax.axis_size("sp")
    fs = lax.axis_size("fs")
    devices = tp * sp * fs
    my_tp = lax.axis_index("tp")
    my_sp = lax.axis_index("sp")
    ring = Ring(tp)
    local_rows, width = tokens.shape[1:]
    heads = width // HD
    my_heads = heads // tp
    head_cols = my_heads * HD
    group_rows = tp * local_rows

    offsets = jnp.arange(BLK, dtype=jnp.int32)
    seg_all = jnp.repeat(block_seg[0], BLK).reshape(tp, sp, local_rows)
    pos_all = (block_pos[0][:, None] + offsets[None, :]).reshape(tp, sp, local_rows)
    query_seg = lax.dynamic_index_in_dim(seg_all, my_sp, 1, keepdims=False).reshape(-1)
    query_pos = lax.dynamic_index_in_dim(pos_all, my_sp, 1, keepdims=False).reshape(-1)
    key_seg = seg_all.transpose(1, 0, 2).reshape(-1)
    key_pos = pos_all.transpose(1, 0, 2).reshape(-1)

    small = [ln1_gain, ln1_bias, b_out, ln2_gain, ln2_bias, b_down, b_qv, b_in]
    sizes = [v.shape[0] for v in small]
    gathered = lax.all_gather(jnp.concatenate(small), EVERY, axis=0, tiled=True)
    gathered = full(half(gathered)).reshape(devices, -1)
    cuts = [sum(sizes[:i]) for i in range(len(sizes) + 1)]
    gain1, bias1, out_bias, gain2, bias2, down_bias, qv_bias, in_bias = (
        gathered[:, cuts[i] : cuts[i + 1]].reshape(-1) for i in range(len(sizes))
    )
    qv_bias = lax.dynamic_slice_in_dim(qv_bias.reshape(2, width), my_tp * head_cols, head_cols, 1)
    in_bias = lax.dynamic_slice_in_dim(in_bias, my_tp * (in_bias.shape[0] // tp), in_bias.shape[0] // tp)

    qkv_slice = columns_in(half(w_qkv), 3, tp)
    out_slice = lax.all_gather(half(w_out), TOKENS, axis=0, tiled=True)
    group_tokens = ring.gather(tokens[0])
    in_slice = columns_in(half(w_in), 1, tp)
    down_slice = lax.all_gather(half(w_down), TOKENS, axis=0, tiled=True)
    group_cot = ring.gather(cotangent[0])

    group_normed, unused_scale = normalize(full(group_tokens))
    normed_half = half(group_normed * gain1 + bias1)
    mixed = dot(normed_half, qkv_slice, 1, 0)
    query = half(mixed[:, :head_cols] + qv_bias[0])
    key = half(mixed[:, head_cols : 2 * head_cols])
    value = half(mixed[:, 2 * head_cols :] + qv_bias[1])

    def by_head(rows):
        return rows.reshape(-1, my_heads, HD)

    query_heads = by_head(query)
    key_heads, value_heads = by_head(key), by_head(value)
    if sp > 1:
        key_heads = lax.all_gather(key_heads, "sp", axis=0, tiled=True)
        value_heads = lax.all_gather(value_heads, "sp", axis=0, tiled=True)
    head_ids = my_tp * my_heads + jnp.arange(my_heads, dtype=jnp.int32)
    slopes = jnp.exp2(-8.0 * (head_ids.astype(jnp.float32) + 1.0) / heads)
    scale_qk = 1.0 / math.sqrt(HD)
    visible = ((key_seg[None, :] == 0) | (key_seg[None, :] == query_seg[:, None])) & (
        key_pos[None, :] <= query_pos[:, None]
    )
    distance = (query_pos[:, None] - key_pos[None, :]).astype(jnp.float32)
    scores = jnp.einsum("qhd,khd->hqk", query_heads, key_heads, preferred_element_type=jnp.float32)
    scores = scores * scale_qk - slopes[:, None, None] * distance[None]
    scores = jnp.where(visible[None], scores, NEG_FILL)
    top = jnp.max(scores, axis=-1, keepdims=True)
    expon = jnp.exp(scores - top)
    probs = expon / jnp.sum(expon, axis=-1, keepdims=True)
    probs_half = half(probs)
    attended = jnp.einsum(
        "hqk,khd->qhd", probs_half, value_heads, preferred_element_type=jnp.float32
    )
    attended = half(attended.reshape(group_rows, head_cols))
    branch = ring.reduce_scatter(dot(attended, out_slice, 1, 0, jnp.bfloat16))
    residual = full(tokens[0]) + branch + out_bias

    own_normed2, scale2 = normalize(residual)
    second = ring.gather(half(own_normed2 * gain2 + bias2))
    pre_act = dot(second, in_slice, 1, 0) + in_bias
    d_act = dot(group_cot, down_slice, 1, 1)
    act, gelu_back = jax.vjp(lambda v: jax.nn.gelu(v, approximate=True), pre_act)
    act = half(act)
    d_pre_full = gelu_back(d_act)[0]
    d_pre = half(d_pre_full)
    d_second = ring.reduce_scatter(dot(d_pre, in_slice, 1, 1, jnp.bfloat16))
    ffn = ring.reduce_scatter(dot(act, down_slice, 1, 0, jnp.bfloat16))
    output = half(residual + ffn + down_bias)
    grad_down_slice = dot(act, group_cot, 0, 0, jnp.bfloat16)
    grad_in_slice = dot(second, d_pre, 0, 0, jnp.bfloat16)
    grad_w_down = full(lax.psum_scatter(grad_down_slice, TOKENS, scatter_dimension=0, tiled=True))
    grad_w_in = columns_out(grad_in_slice, 1, tp)
    grad_b_in = jnp.sum(full(d_pre), axis=0)

    own_cot = full(cotangent[0])
    d_residual = own_cot + normalize_back(own_normed2, scale2, d_second * gain2)
    d_branch_own = half(d_residual)
    d_branch = ring.gather(d_branch_own)

    grad_out_slice = dot(attended, d_branch, 0, 0, jnp.bfloat16)
    grad_w_out = full(lax.psum_scatter(grad_out_slice, TOKENS, scatter_dimension=0, tiled=True))
    d_attended = by_head(dot(d_branch, out_slice, 1, 1, jnp.bfloat16))
    d_prob = jnp.einsum(
        "qhd,khd->hqk", d_attended, value_heads, preferred_element_type=jnp.float32
    )
    delta = jnp.sum(probs * d_prob, axis=-1, keepdims=True)
    d_score = half(probs * (d_prob - delta))
    d_query = jnp.einsum("hqk,khd->qhd", d_score, key_heads, preferred_element_type=jnp.float32)
    d_key = jnp.einsum("hqk,qhd->khd", d_score, query_heads, preferred_element_type=jnp.float32)
    d_value = jnp.einsum(
        "hqk,qhd->khd", probs_half, d_attended, preferred_element_type=jnp.float32
    )
    if sp > 1:
        d_key = lax.psum_scatter(d_key, "sp", scatter_dimension=0, tiled=True)
        d_value = lax.psum_scatter(d_value, "sp", scatter_dimension=0, tiled=True)
    d_query = half((d_query * scale_qk).reshape(group_rows, head_cols))
    d_key = half((d_key * scale_qk).reshape(group_rows, head_cols))
    d_value = half(d_value.reshape(group_rows, head_cols))
    d_mixed = jnp.concatenate([d_query, d_key, d_value], axis=1)
    d_normed_partial = dot(d_mixed, qkv_slice, 1, 1)
    d_normed = ring.reduce_scatter(half(d_normed_partial))
    grad_w_qkv = columns_out(dot(normed_half, d_mixed, 0, 0, jnp.bfloat16), 3, tp)

    own_normed1, scale1 = normalize(full(tokens[0]))
    grad_tokens = d_residual + normalize_back(own_normed1, scale1, d_normed * gain1)

    def placed(values, whole):
        start = my_tp * values.shape[-1]
        blank = jnp.zeros(values.shape[:-1] + (whole,), jnp.float32)
        return lax.dynamic_update_slice_in_dim(blank, values, start, values.ndim - 1)

    grad_b_qv = placed(
        jnp.stack([jnp.sum(full(d_query), axis=0), jnp.sum(full(d_value), axis=0)]), width
    )
    partials = [
        jnp.sum(d_normed_partial * group_normed, axis=0),
        jnp.sum(d_normed_partial, axis=0),
        jnp.sum(full(d_branch_own), axis=0),
        jnp.sum(d_second * own_normed2, axis=0),
        jnp.sum(d_second, axis=0),
        jnp.sum(own_cot, axis=0),
        grad_b_qv.reshape(-1),
        placed(grad_b_in, tp * grad_b_in.shape[0]),
    ]
    stacked = jnp.concatenate([v.reshape(devices, -1) for v in partials], axis=1)
    summed = lax.psum_scatter(stacked, EVERY, scatter_dimension=0, tiled=True).reshape(-1)
    g_gain1, g_bias1, g_b_out, g_gain2, g_bias2, g_b_down, g_b_qv, g_b_in = (
        summed[cuts[i] : cuts[i + 1]] for i in range(len(sizes))
    )
    return (
        output[None],
        grad_tokens[None],
        g_gain1,
        g_bias1,
        grad_w_qkv,
        g_b_qv,
        grad_w_out,
        g_b_out,
        g_gain2,
        g_bias2,
        grad_w_in,
        g_b_in,
        grad_w_down,
        g_b_down,
    )


def solution(mesh):
    ctx, fs = mesh.shape["ctx"], mesh.shape["fsdp"]
    tp = math.gcd(ctx, len(SNAKE))
    inner = Mesh(mesh.devices.reshape(tp, ctx // tp, fs), EVERY)
    rows = P("fs", ("tp", "sp"), None)
    vector, matrix, blocks = P(EVERY), P(EVERY, None), P("fs", None)
    return jax.shard_map(
        on_device,
        mesh=inner,
        in_specs=(
            rows,
            vector,
            vector,
            matrix,
            vector,
            matrix,
            vector,
            vector,
            vector,
            matrix,
            vector,
            matrix,
            vector,
            rows,
            blocks,
            blocks,
        ),
        out_specs=(
            rows,
            rows,
            vector,
            vector,
            matrix,
            vector,
            matrix,
            vector,
            vector,
            vector,
            matrix,
            vector,
            matrix,
            vector,
        ),
        check_vma=False,
    )
```

```python
import functools
import math

import jax
import jax.numpy as jnp
from jax import lax
from jax.experimental import pallas as pl
from jax.experimental.pallas import tpu as pltpu
from jax.sharding import Mesh
from jax.sharding import PartitionSpec as P

HD = 128
BLK = 128
EPSILON = 1e-05
NEG_FILL = -1e30

EVERY = ("tp", "sp", "fs")
TOKENS = ("sp", "fs")
SNAKE = (0, 2, 4, 6, 7, 5, 3, 1)
PLACES = len(SNAKE)
SHIFTS = (0, -1, 1, -2, 2, -3, 3, 4)
PARTS = ((0, 1), (1, 3), (3, 5), (5, 7), (7, 8))


def half(values):
    return values.astype(jnp.bfloat16)


def full(values):
    return values.astype(jnp.float32)


def dot(left, right, left_dim, right_dim, out=jnp.float32):
    return lax.dot_general(
        left, right, (((left_dim,), (right_dim,)), ((), ())), preferred_element_type=jnp.float32
    ).astype(out)


def fence(*values):
    return lax.optimization_barrier(values)


def normalize(values):
    center = values - jnp.mean(values, axis=-1, keepdims=True)
    spread = jnp.mean(center * center, axis=-1, keepdims=True)
    scale = lax.rsqrt(spread + EPSILON)
    return center * scale, scale


def normalize_back(normed, scale, grad):
    return scale * (
        grad
        - jnp.mean(grad, axis=-1, keepdims=True)
        - normed * jnp.mean(grad * normed, axis=-1, keepdims=True)
    )


def hop(upward, downward):
    up = [(SNAKE[i], SNAKE[(i + 1) % PLACES]) for i in range(PLACES)]
    down = [(b, a) for a, b in up]
    return lax.ppermute(upward, "tp", up), lax.ppermute(downward, "tp", down)


def last_hop(below, above):
    n = below.shape[0] // 2
    return hop(below[:n], above[n:])


def first_sum(part, low, high):
    below, above = jnp.split(part, 2)
    n = below.shape[0] // 2
    upward = jnp.concatenate([half(full(above[:n]) + full(low)), above[n:]])
    downward = jnp.concatenate([below[:n], half(full(below[n:]) + full(high))])
    return upward, downward


def next_sum(part, upward, downward):
    below, above = jnp.split(part, 2)
    return half(full(above) + full(upward)), half(full(below) + full(downward))


def last_sum(part, upward, downward):
    return full(part) + full(upward) + full(downward)


def join(pair):
    return jnp.concatenate(pair)


def put(buffer, part, index, local_rows):
    return lax.dynamic_update_slice_in_dim(buffer, part, PARTS[index][0] * local_rows, 0)


def bits_of(names):
    return [
        (name, 1 << bit, lax.axis_size(name))
        for name in reversed(names)
        for bit in range(lax.axis_size(name).bit_length() - 1)
    ]


def swap(values, name, bit, size):
    return lax.ppermute(values, name, [(i, i ^ bit) for i in range(size)])


def gather_small(values):
    values = values[None]
    for name, bit, size in bits_of(EVERY):
        other = swap(values, name, bit, size)
        first = (lax.axis_index(name) & bit) == 0
        values = jnp.concatenate([jnp.where(first, values, other), jnp.where(first, other, values)])
    return values


def sum_small(values):
    for name, bit, size in bits_of(EVERY):
        values = values.reshape(-1, 2, values.shape[-1])
        low, high = values[:, 0], values[:, 1]
        first = (lax.axis_index(name) & bit) == 0
        other = swap(jnp.where(first, high, low), name, bit, size)
        values = jnp.where(first, low, high) + other
    return values[0]


def by_place(rows, groups):
    n, width = rows.shape
    part = width // groups // PLACES
    rows = half(rows).reshape(n, groups, PLACES, part).transpose(2, 0, 1, 3)
    return rows.reshape(PLACES, n, groups * part)


def exchange(pieces):
    return lax.all_to_all(pieces, "tp", split_axis=0, concat_axis=0, tiled=True)


def rows_product(lefts, rights, tile, name):
    count, out_rows, out_cols = len(lefts), lefts[0].shape[1], rights[0].shape[1]

    def body(*refs):
        total = None
        for left, right in zip(refs[:count], refs[count : 2 * count], strict=True):
            term = lax.dot_general(
                left[...],
                right[...],
                (((0,), (0,)), ((), ())),
                preferred_element_type=jnp.float32,
            )
            total = term if total is None else total + term
        refs[2 * count][...] = half(total)

    return pl.pallas_call(
        body,
        grid=(out_rows // tile,),
        in_specs=[pl.BlockSpec((v.shape[0], tile), lambda i: (0, i)) for v in lefts]
        + [pl.BlockSpec(v.shape, lambda i: (0, 0)) for v in rights],
        out_specs=pl.BlockSpec((tile, out_cols), lambda i: (i, 0)),
        out_shape=jax.ShapeDtypeStruct((out_rows, out_cols), jnp.bfloat16),
        compiler_params=pltpu.CompilerParams(vmem_limit_bytes=40 << 20),
        cost_estimate=pl.CostEstimate(flops=1 << 20, bytes_accessed=1 << 20, transcendentals=0),
        name=name,
    )(*lefts, *rights)


def score_rows(keys, queries, slope, first_block, query_pos, query_seg, key_pos, key_seg):
    scores = dot(keys, queries, 1, 1)
    count = queries.shape[0] // BLK
    lane = lax.broadcasted_iota(jnp.int32, (1, queries.shape[0]), 1)
    down = lax.broadcasted_iota(jnp.int32, (BLK, queries.shape[0]), 0)
    ahead = down - lax.rem(lane, BLK)
    slant = slope * full(down)
    tiles = []
    for j in range(keys.shape[0] // BLK):
        limit = jnp.zeros((1, queries.shape[0]), jnp.int32)
        for i in range(count):
            block = first_block * count + i
            seen = (key_seg[j] == 0) | (key_seg[j] == query_seg[block])
            here = jnp.where(seen, query_pos[block] - key_pos[j], -BLK)
            limit = jnp.where(lane >= i * BLK, here, limit)
        tile = scores[j * BLK : (j + 1) * BLK] * (1.0 / math.sqrt(HD))
        tile = tile + (slant + slope * full(key_pos[j]))
        tiles.append(jnp.where(ahead <= limit, tile, NEG_FILL))
    return jnp.concatenate(tiles)


def attend_body(
    query_pos, query_seg, key_pos, key_seg, slopes, query, key, value, attended, level, value_t
):
    @pl.when(pl.program_id(1) == 0)
    def turn():
        value_t[...] = half(full(value[...]).T)

    scores = score_rows(
        key[...],
        query[...],
        slopes[pl.program_id(0)],
        pl.program_id(1),
        query_pos,
        query_seg,
        key_pos,
        key_seg,
    )
    top = jnp.max(scores, axis=0, keepdims=True)
    expon = jnp.exp(scores - top)
    total = jnp.sum(expon, axis=0, keepdims=True)
    probs = half(expon * (1.0 / total))
    attended[...] = half(dot(value_t[...], probs, 1, 0).T)
    level[...] = (top + jnp.log(total))[None]


def attend_back_body(
    my_heads,
    split,
    query_pos,
    query_seg,
    key_pos,
    key_seg,
    slopes,
    query,
    key,
    value,
    grad,
    level,
    *rest,
):
    d_query, d_keys = (rest[0], rest[1]) if split else (rest[0], rest[0])
    key_t, key_acc, value_acc = rest[-3:]
    head, block = pl.program_id(0), pl.program_id(1)
    rows = query.shape[0]
    scale = 1.0 / math.sqrt(HD)

    def columns(place):
        return pl.ds(pl.multiple_of((place * my_heads + head) * HD, HD), HD)

    @pl.when(block == 0)
    def begin():
        key_t[...] = half(full(key[...]).T)
        key_acc[...] = jnp.zeros_like(key_acc)
        value_acc[...] = jnp.zeros_like(value_acc)

    scores = score_rows(
        key[...], query[...], slopes[head], block, query_pos, query_seg, key_pos, key_seg
    )
    probs = jnp.exp(scores - level[0])
    d_probs = dot(value[...], grad[...], 1, 1)
    delta = jnp.sum(probs * d_probs, axis=0, keepdims=True)
    d_scores = half(probs * (d_probs - delta))
    turned = (dot(key_t[...], d_scores, 1, 0) * scale).T
    d_query[pl.ds(pl.multiple_of(block * rows, rows), rows), columns(0)] = half(turned)
    key_acc[...] += dot(d_scores, query[...], 1, 0)
    value_acc[...] += dot(half(probs), grad[...], 1, 0)

    @pl.when(block == pl.num_programs(1) - 1)
    def end():
        shift = 0 if split else 1
        d_keys[:, columns(shift)] = half(key_acc[...] * scale)
        d_keys[:, columns(shift + 1)] = half(value_acc[...])


def attention(blocks, slopes, query, keys, first, grad=None, level=None):
    my_heads = slopes.shape[0]
    rows, total = query.shape[0], keys.shape[0]
    step = 256 if total <= 1024 else BLK
    columns = my_heads * HD
    scalars = pl.BlockSpec(memory_space=pltpu.SMEM)
    of_query = pl.BlockSpec((step, HD), lambda h, i: (i, h))
    of_level = pl.BlockSpec((1, 1, step), lambda h, i: (h, 0, i))
    in_specs = [scalars] * 5 + [
        of_query,
        pl.BlockSpec((total, HD), lambda h, i: (0, first + h)),
        pl.BlockSpec((total, HD), lambda h, i: (0, first + my_heads + h)),
    ]
    settings = {
        "grid": (my_heads, rows // step),
        "compiler_params": pltpu.CompilerParams(vmem_limit_bytes=48 << 20),
        "cost_estimate": pl.CostEstimate(
            flops=(4 if grad is None else 10) * rows * total * columns,
            bytes_accessed=32 << 20,
            transcendentals=my_heads * rows * total,
        ),
    }
    if grad is None:
        return pl.pallas_call(
            attend_body,
            in_specs=in_specs,
            out_specs=[of_query, of_level],
            out_shape=[
                jax.ShapeDtypeStruct((rows, columns), jnp.bfloat16),
                jax.ShapeDtypeStruct((my_heads, 1, rows), jnp.float32),
            ],
            scratch_shapes=[pltpu.VMEM((HD, total), jnp.bfloat16)],
            name="attend",
            **settings,
        )(*blocks, slopes, query, keys, keys)
    split = query is not keys
    shapes = [(rows, columns), (total, 2 * columns)] if split else [(rows, 3 * columns)]
    return pl.pallas_call(
        functools.partial(attend_back_body, my_heads, split),
        in_specs=in_specs + [of_query, of_level],
        out_specs=[pl.BlockSpec(shape, lambda h, i: (0, 0)) for shape in shapes],
        out_shape=[jax.ShapeDtypeStruct(shape, jnp.bfloat16) for shape in shapes],
        scratch_shapes=[
            pltpu.VMEM((HD, total), jnp.bfloat16),
            pltpu.VMEM((total, HD), jnp.float32),
            pltpu.VMEM((total, HD), jnp.float32),
        ],
        name="attend_back",
        **settings,
    )(*blocks, slopes, query, keys, keys, grad, level)


def products(parts, matrix, name):
    count, tile = len(parts), 512

    def body(*refs):
        for part, out in zip(refs[:count], refs[count + 1 :], strict=True):
            out[...] = dot(part[...], refs[count][...], 1, 1, jnp.bfloat16)

    return pl.pallas_call(
        body,
        grid=(matrix.shape[0] // tile,),
        in_specs=[pl.BlockSpec(v.shape, lambda i: (0, 0)) for v in parts]
        + [pl.BlockSpec((tile, matrix.shape[1]), lambda i: (i, 0))],
        out_specs=[pl.BlockSpec((v.shape[0], tile), lambda i: (0, i)) for v in parts],
        out_shape=[
            jax.ShapeDtypeStruct((v.shape[0], matrix.shape[0]), jnp.bfloat16) for v in parts
        ],
        compiler_params=pltpu.CompilerParams(vmem_limit_bytes=40 << 20),
        cost_estimate=pl.CostEstimate(flops=1 << 20, bytes_accessed=1 << 20, transcendentals=0),
        name=name,
    )(*parts, matrix)


def gather_rows(rows):
    rows = lax.all_gather(rows, TOKENS, axis=1, tiled=True)
    return rows.reshape(-1, rows.shape[2])


def from_places(grad, groups):
    places, n, width = grad.shape
    grad = grad.reshape(places, n, groups, width // groups).transpose(1, 2, 0, 3)
    return full(grad.reshape(n, places * width))


def on_device(
    tokens,
    ln1_gain,
    ln1_bias,
    w_qkv,
    b_qv,
    w_out,
    b_out,
    ln2_gain,
    ln2_bias,
    w_in,
    b_in,
    w_down,
    b_down,
    cotangent,
    block_seg,
    block_pos,
):
    sp = lax.axis_size("sp")
    fs = lax.axis_size("fs")
    devices = PLACES * sp * fs
    my_tp = lax.axis_index("tp")
    my_sp = lax.axis_index("sp")
    local_rows, width = tokens.shape[1:]
    heads = width // HD
    my_heads = heads // PLACES
    head_cols = my_heads * HD
    hidden = w_in.shape[1] // PLACES
    group_rows = PLACES * local_rows

    def buffer(columns):
        return jnp.zeros((group_rows, columns), jnp.bfloat16)

    def by_part(rows):
        return [rows[a * local_rows : b * local_rows] for a, b in PARTS]

    order = [[SNAKE[(SNAKE.index(i) + s) % PLACES] for s in SHIFTS] for i in range(PLACES)]
    sources = jnp.asarray(order, jnp.int32)[my_tp]
    picked = (sources[:, None] == jnp.arange(PLACES, dtype=jnp.int32)[None, :]).astype(jnp.int32)

    def in_order(blocks):
        blocks = jnp.sum(picked[:, :, None, None] * blocks.reshape(1, PLACES, sp, -1), axis=1)
        mine = lax.dynamic_index_in_dim(blocks, my_sp, 1, keepdims=False).reshape(-1)
        return mine, blocks.transpose(1, 0, 2).reshape(-1)

    query_seg, key_seg = in_order(block_seg[0])
    query_pos, key_pos = in_order(block_pos[0])
    blocks = (query_pos, query_seg, key_pos, key_seg)
    head_ids = my_tp * my_heads + jnp.arange(my_heads, dtype=jnp.int32)
    slopes = jnp.exp2(-8.0 * (head_ids.astype(jnp.float32) + 1.0) / heads)

    small = [ln1_gain, ln1_bias, b_out, ln2_gain, ln2_bias, b_down, b_qv, b_in]
    sizes = [v.shape[0] for v in small]
    cuts = [sum(sizes[:i]) for i in range(len(sizes) + 1)]
    own, own_cot = tokens[0], cotangent[0]

    low1, high1 = hop(own, own)
    down_slice = lax.all_gather(half(w_down), TOKENS, axis=0, tiled=True)
    small_own, qkv_pieces = fence(half(jnp.concatenate(small)), by_place(w_qkv, 3))
    qkv_pieces = exchange(qkv_pieces)
    gathered = gather_small(small_own)
    low2, high2 = hop(low1, high1)
    in_pieces = by_place(w_in, 1)
    (
        low1,
        high1,
        low2,
        high2,
        qkv_pieces,
        in_pieces,
        gathered,
        down_slice,
        w_out,
        own_cot,
    ) = fence(
        low1,
        high1,
        low2,
        high2,
        qkv_pieces,
        in_pieces,
        gathered,
        down_slice,
        w_out,
        own_cot,
    )
    gathered = full(gathered)
    gain1, bias1, out_bias, gain2, bias2, down_bias, qv_bias, in_bias = (
        gathered[:, cuts[i] : cuts[i + 1]].reshape(-1) for i in range(len(sizes))
    )
    qv_bias = lax.dynamic_slice_in_dim(qv_bias.reshape(2, width), my_tp * head_cols, head_cols, 1)
    in_bias = lax.dynamic_slice_in_dim(in_bias, my_tp * hidden, hidden)

    def norm1(rows):
        return half(normalize(full(rows))[0] * gain1 + bias1)

    in_pieces = exchange(in_pieces)
    qkv_slice = gather_rows(qkv_pieces)
    out_slice = lax.all_gather(half(w_out), TOKENS, axis=0, tiled=True)
    token_parts = [own, join((low1, high1)), join((low2, high2))]
    low3, high3 = hop(low2, high2)
    normed = [norm1(part) for part in token_parts]
    low3, high3, own_cot, *normed = fence(low3, high3, own_cot, *normed)
    low4, high4 = last_hop(low3, high3)
    token_parts.append(join((low3, high3)))
    normed.append(norm1(token_parts[3]))
    low4, high4, own_cot, in_pieces, qkv_slice, *normed = fence(
        low4, high4, own_cot, in_pieces, qkv_slice, *normed
    )

    cot_low1, cot_high1 = hop(own_cot, own_cot)
    token_parts.append(join((low4, high4)))
    normed.append(norm1(token_parts[4]))
    blank = jnp.zeros((head_cols,), jnp.float32)
    qkv_bias = jnp.concatenate([qv_bias[0], blank, qv_bias[1]])
    mixed = jnp.concatenate([half(dot(part, qkv_slice, 1, 0) + qkv_bias) for part in normed])
    mixed, cot_low1, cot_high1, out_slice = fence(mixed, cot_low1, cot_high1, out_slice)
    in_slice = gather_rows(in_pieces)
    cot_low2, cot_high2 = hop(cot_low1, cot_high1)
    keys = mixed
    if sp > 1:
        keys = lax.all_gather(mixed[:, head_cols:], "sp", axis=0, tiled=True)
    first_key = my_heads if sp == 1 else 0
    attended, level = attention(blocks, slopes, mixed, keys, first_key)
    attended, cot_low2, cot_high2 = fence(attended, cot_low2, cot_high2)

    attended_parts = by_part(attended)
    branch_parts = [dot(attended_parts[i], out_slice, 1, 0, jnp.bfloat16) for i in range(5)]
    branch_low, branch_high = hop(*jnp.split(branch_parts[4], 2))
    cot_low3, cot_high3 = hop(cot_low2, cot_high2)
    branch_low, branch_high, cot_low3, cot_high3, *branch_parts = fence(
        branch_low, branch_high, cot_low3, cot_high3, *branch_parts
    )
    up, down = hop(*first_sum(branch_parts[3], branch_low, branch_high))
    cot_low4, cot_high4 = last_hop(cot_low3, cot_high3)
    up, down, cot_low4, cot_high4, in_slice = fence(up, down, cot_low4, cot_high4, in_slice)
    up, down = hop(*next_sum(branch_parts[2], up, down))
    cot_parts = [own_cot, join((cot_low1, cot_high1)), join((cot_low2, cot_high2))]
    cot_parts += [join((cot_low3, cot_high3)), join((cot_low4, cot_high4))]
    up, down, *cot_parts = fence(up, down, *cot_parts)
    up, down = fence(*hop(*next_sum(branch_parts[1], up, down)))
    residual = full(own) + last_sum(branch_parts[0], up, down) + out_bias

    own_normed2, scale2 = normalize(residual)
    second = half(own_normed2 * gain2 + bias2)
    second_parts, act_parts, d_pre_parts, d_second_parts, ffn_parts = [second], [], [], [], []
    low, high = second, second
    for index in range(5):
        if index < 3:
            new_low, new_high = hop(low, high)
        elif index == 3:
            new_low, new_high = last_hop(low, high)
        if index:
            second_parts.append(join((low, high)))
        pre_act = dot(second_parts[index], in_slice, 1, 0) + in_bias
        act, gelu_back = jax.vjp(lambda v: jax.nn.gelu(v, approximate=True), pre_act)
        act_parts.append(half(act))
        d_pre = half(gelu_back(dot(cot_parts[index], down_slice, 1, 1))[0])
        d_pre_parts.append(d_pre)
        d_second_parts.append(dot(d_pre, in_slice, 1, 1, jnp.bfloat16))
        made = [act_parts, d_pre_parts, d_second_parts]
        if index < 3:
            ffn_parts.append(dot(act_parts[index], down_slice, 1, 0, jnp.bfloat16))
            made.append(ffn_parts)
        if index < 4:
            low, high, *held = fence(new_low, new_high, *[parts[index] for parts in made])
            for parts, value in zip(made, held, strict=True):
                parts[index] = value

    low, high = hop(*jnp.split(d_second_parts[4], 2))
    ffn_parts += [dot(act, down_slice, 1, 0, jnp.bfloat16) for act in act_parts[3:]]
    low, high, d_pre_parts[4], act_parts[4], *ffn_parts = fence(
        low, high, d_pre_parts[4], act_parts[4], *ffn_parts
    )
    up, down = hop(*first_sum(d_second_parts[3], low, high))
    out_up, out_down = hop(*jnp.split(ffn_parts[4], 2))
    grad_in = rows_product(second_parts, d_pre_parts, 512, "grad_in")
    grad_in = grad_in.reshape(PLACES, -1, hidden)
    up, down, out_up, out_down, grad_in = fence(up, down, out_up, out_down, grad_in)
    grad_in = lax.psum_scatter(grad_in, TOKENS, scatter_dimension=1, tiled=True)
    up, down = hop(*next_sum(d_second_parts[2], up, down))
    out_up, out_down = hop(*first_sum(ffn_parts[3], out_up, out_down))
    up, down, out_up, out_down, act_parts[4] = fence(up, down, out_up, out_down, act_parts[4])
    up, down = hop(*next_sum(d_second_parts[1], up, down))
    out_up, out_down = hop(*next_sum(ffn_parts[2], out_up, out_down))
    grad_down = rows_product(act_parts, cot_parts, 256, "grad_down")
    grad_b_in = sum(jnp.sum(full(part), axis=0) for part in d_pre_parts)
    up, down, out_up, out_down, grad_down, grad_b_in = fence(
        up, down, out_up, out_down, grad_down, grad_b_in
    )
    grad_down = lax.psum_scatter(grad_down, TOKENS, scatter_dimension=0, tiled=True)
    d_second = last_sum(d_second_parts[0], up, down)

    d_residual = full(own_cot) + normalize_back(own_normed2, scale2, d_second * gain2)
    d_branch = half(d_residual)
    low, high = hop(d_branch, d_branch)
    out_up, out_down = hop(*next_sum(ffn_parts[1], out_up, out_down))
    low, high, out_up, out_down = fence(low, high, out_up, out_down)
    d_branch_parts, d_attended = [d_branch], [dot(d_branch, out_slice, 1, 1, jnp.bfloat16)]
    for index in range(1, 5):
        d_branch_parts.append(join((low, high)))
        d_attended.append(dot(d_branch_parts[index], out_slice, 1, 1, jnp.bfloat16))
        if index < 3:
            low, high = hop(low, high)
            low, high, grad_in, d_attended[index] = fence(low, high, grad_in, d_attended[index])
        elif index == 3:
            low, high = last_hop(low, high)
            low, high, grad_in, d_attended[index] = fence(low, high, grad_in, d_attended[index])
            grad_in = exchange(grad_in)

    d_attended = jnp.concatenate(d_attended)
    grads = attention(blocks, slopes, mixed, keys, first_key, d_attended, level)
    if sp == 1:
        (d_mixed,) = grads
    else:
        d_keys = half(lax.psum_scatter(full(grads[1]), "sp", scatter_dimension=0, tiled=True))
        d_mixed = jnp.concatenate([grads[0], d_keys], axis=1)
    d_mixed, d_branch_parts[4], grad_down = fence(d_mixed, d_branch_parts[4], grad_down)

    mixed_parts = by_part(d_mixed)
    far = dot(mixed_parts[4], qkv_slice, 1, 1, jnp.bfloat16)
    low, high = hop(*jnp.split(far, 2))
    near = dot(mixed_parts[3], qkv_slice, 1, 1, jnp.bfloat16)
    grad_qkv = rows_product(normed, mixed_parts, 512, "grad_qkv")
    grad_qkv = grad_qkv.reshape(PLACES, -1, 3 * head_cols)
    low, high, grad_qkv, near, grad_in = fence(low, high, grad_qkv, near, grad_in)
    grad_qkv = lax.psum_scatter(grad_qkv, TOKENS, scatter_dimension=1, tiled=True)
    up, down = hop(*first_sum(near, low, high))
    d_normed = products(mixed_parts[:3], qkv_slice, "d_normed")
    up, down, attended_parts[4], *d_normed = fence(up, down, attended_parts[4], *d_normed)
    up, down = hop(*next_sum(d_normed[2], up, down))
    grad_out = rows_product(attended_parts, d_branch_parts, 128, "grad_out")
    up, down, grad_out = fence(up, down, grad_out)
    grad_qkv, grad_out = fence(grad_qkv, grad_out)
    grad_out = lax.psum_scatter(grad_out, TOKENS, scatter_dimension=0, tiled=True)
    up, down = hop(*next_sum(d_normed[1], up, down))
    up, down, grad_qkv, grad_in, grad_down, out_up, out_down = fence(
        up, down, grad_qkv, grad_in, grad_down, out_up, out_down
    )
    grad_qkv = exchange(grad_qkv)
    d_normed_own = last_sum(d_normed[0], up, down)
    own_normed1, scale1 = normalize(full(own))
    grad_tokens = d_residual + normalize_back(own_normed1, scale1, d_normed_own * gain1)
    grad_w_in = from_places(grad_in, 1)
    grad_w_down = full(grad_down)
    output = half(residual + last_sum(ffn_parts[0], out_up, out_down) + down_bias)

    def placed(values, whole):
        start = my_tp * values.shape[-1]
        blank = jnp.zeros(values.shape[:-1] + (whole,), jnp.float32)
        return lax.dynamic_update_slice_in_dim(blank, values, start, values.ndim - 1)

    mixed_sum = jnp.sum(full(d_mixed), axis=0)
    grad_b_qv = placed(
        jnp.stack([mixed_sum[:head_cols], mixed_sum[2 * head_cols :]]), width
    )
    partials = [
        jnp.sum(d_normed_own * own_normed1, axis=0),
        jnp.sum(d_normed_own, axis=0),
        jnp.sum(full(d_branch), axis=0),
        jnp.sum(d_second * own_normed2, axis=0),
        jnp.sum(d_second, axis=0),
        jnp.sum(full(own_cot), axis=0),
        grad_b_qv.reshape(-1),
        placed(grad_b_in, PLACES * hidden),
    ]
    stacked = jnp.concatenate([v.reshape(devices, -1) for v in partials], axis=1)
    summed = sum_small(stacked)
    grad_w_out = full(grad_out)
    grad_w_qkv = from_places(grad_qkv, 3)
    g_gain1, g_bias1, g_b_out, g_gain2, g_bias2, g_b_down, g_b_qv, g_b_in = (
        summed[cuts[i] : cuts[i + 1]] for i in range(len(sizes))
    )
    return (
        output[None],
        grad_tokens[None],
        g_gain1,
        g_bias1,
        grad_w_qkv,
        g_b_qv,
        grad_w_out,
        g_b_out,
        g_gain2,
        g_bias2,
        grad_w_in,
        g_b_in,
        grad_w_down,
        g_b_down,
    )


def solution(mesh):
    ctx, fs = mesh.shape["ctx"], mesh.shape["fsdp"]
    inner = Mesh(mesh.devices.reshape(PLACES, ctx // PLACES, fs), EVERY)
    rows = P("fs", ("tp", "sp"), None)
    vector, matrix, blocks = P(EVERY), P(EVERY, None), P("fs", None)
    kinds = (
        rows,
        vector,
        vector,
        matrix,
        vector,
        matrix,
        vector,
        vector,
        vector,
        matrix,
        vector,
        matrix,
        vector,
    )
    return jax.shard_map(
        on_device,
        mesh=inner,
        in_specs=kinds + (rows, blocks, blocks),
        out_specs=(rows,) + kinds,
        check_vma=False,
    )
```

```python
import functools
import math

import jax
import jax.numpy as jnp
from jax import lax
from jax.experimental import pallas as pl
from jax.experimental.pallas import tpu as pltpu
from jax.sharding import Mesh
from jax.sharding import PartitionSpec as P

HD = 128
BLK = 128
EPSILON = 1e-05
NEG_FILL = -1e30

EVERY = ("tp", "sp", "fs")
TOKENS = ("sp", "fs")
SNAKE = (0, 2, 4, 6, 7, 5, 3, 1)
PLACES = len(SNAKE)
SHIFTS = (0, -1, 1, -2, 2, -3, 3, 4)
PARTS = ((0, 1), (1, 3), (3, 5), (5, 7), (7, 8))


def half(values):
    return values.astype(jnp.bfloat16)


def full(values):
    return values.astype(jnp.float32)


def dot(left, right, left_dim, right_dim, out=jnp.float32):
    return lax.dot_general(
        left, right, (((left_dim,), (right_dim,)), ((), ())), preferred_element_type=jnp.float32
    ).astype(out)


def fence(*values):
    return lax.optimization_barrier(values)


def normalize(values):
    center = values - jnp.mean(values, axis=-1, keepdims=True)
    spread = jnp.mean(center * center, axis=-1, keepdims=True)
    scale = lax.rsqrt(spread + EPSILON)
    return center * scale, scale


def normalize_back(normed, scale, grad):
    return scale * (
        grad
        - jnp.mean(grad, axis=-1, keepdims=True)
        - normed * jnp.mean(grad * normed, axis=-1, keepdims=True)
    )


def hop(upward, downward):
    up = [(SNAKE[i], SNAKE[(i + 1) % PLACES]) for i in range(PLACES)]
    down = [(b, a) for a, b in up]
    return lax.ppermute(upward, "tp", up), lax.ppermute(downward, "tp", down)


def last_hop(below, above):
    n = below.shape[0] // 2
    return hop(below[:n], above[n:])


def first_sum(part, low, high):
    below, above = jnp.split(part, 2)
    n = below.shape[0] // 2
    upward = jnp.concatenate([half(full(above[:n]) + full(low)), above[n:]])
    downward = jnp.concatenate([below[:n], half(full(below[n:]) + full(high))])
    return upward, downward


def next_sum(part, upward, downward):
    below, above = jnp.split(part, 2)
    return half(full(above) + full(upward)), half(full(below) + full(downward))


def last_sum(part, upward, downward):
    return full(part) + full(upward) + full(downward)


def join(pair):
    return jnp.concatenate(pair)


def put(buffer, part, index, local_rows):
    return lax.dynamic_update_slice_in_dim(buffer, part, PARTS[index][0] * local_rows, 0)


def bits_of(names):
    return [
        (name, 1 << bit, lax.axis_size(name))
        for name in reversed(names)
        for bit in range(lax.axis_size(name).bit_length() - 1)
    ]


def swap(values, name, bit, size):
    return lax.ppermute(values, name, [(i, i ^ bit) for i in range(size)])


def gather_small(values, bits):
    for name, bit, size in bits:
        other = swap(values, name, bit, size)
        first = (lax.axis_index(name) & bit) == 0
        values = jnp.concatenate([jnp.where(first, values, other), jnp.where(first, other, values)])
    return values


def sum_small(values, names):
    for name, bit, size in bits_of(names):
        values = values + swap(values, name, bit, size)
    return values


def by_place(rows, groups):
    n, width = rows.shape
    part = width // groups // PLACES
    rows = half(rows).reshape(n, groups, PLACES, part).transpose(2, 0, 1, 3)
    return rows.reshape(PLACES, n, groups * part)


def exchange(pieces):
    return lax.all_to_all(pieces, "tp", split_axis=0, concat_axis=0, tiled=True)


def in_hbm(*arrays):
    return [pltpu.with_memory_space_constraint(v, pltpu.HBM) for v in arrays]


def settings(name, megabytes=40):
    return {
        "compiler_params": pltpu.CompilerParams(vmem_limit_bytes=megabytes << 20),
        "cost_estimate": pl.CostEstimate(flops=1 << 20, bytes_accessed=1 << 20, transcendentals=0),
        "name": name,
    }


def rows_product(lefts, rights, tile, name):
    count, out_rows, out_cols = len(lefts), lefts[0].shape[1], rights[0].shape[1]

    def body(*refs):
        total = None
        for left, right in zip(refs[:count], refs[count : 2 * count], strict=True):
            term = lax.dot_general(
                left[...],
                right[...],
                (((0,), (0,)), ((), ())),
                preferred_element_type=jnp.float32,
            )
            total = term if total is None else total + term
        refs[2 * count][...] = half(total)

    return pl.pallas_call(
        body,
        grid=(out_rows // tile,),
        in_specs=[pl.BlockSpec((v.shape[0], tile), lambda i: (0, i)) for v in lefts]
        + [pl.BlockSpec(v.shape, lambda i: (0, 0)) for v in rights],
        out_specs=pl.BlockSpec((tile, out_cols), lambda i: (i, 0)),
        out_shape=pltpu.HBM((out_rows, out_cols), jnp.bfloat16),
        **settings(name),
    )(*lefts, *rights)


def score_rows(table, keys, queries, heads, query_blocks):
    scores = dot(keys, queries, 1, 1)
    count, key_blocks = queries.shape[0] // BLK, keys.shape[0] // BLK
    lane = lax.broadcasted_iota(jnp.int32, (1, queries.shape[0]), 1)
    down = lax.broadcasted_iota(jnp.int32, (BLK, queries.shape[0]), 0)
    ahead = down - lax.rem(lane, BLK)
    head = table[2 * query_blocks + 2 * key_blocks] + pl.program_id(0)
    slope = jnp.exp2(full(jnp.full(down.shape, head + 1, jnp.int32)) * (-8.0 / heads))
    slant = slope * full(down)
    tiles = []
    for j in range(key_blocks):
        key_pos = table[2 * query_blocks + j]
        key_seg = table[2 * query_blocks + key_blocks + j]
        limit = jnp.zeros((1, queries.shape[0]), jnp.int32)
        for i in range(count):
            block = pl.program_id(1) * count + i
            seen = (key_seg == 0) | (key_seg == table[query_blocks + block])
            here = jnp.where(seen, table[block] - key_pos, -BLK)
            limit = jnp.where(lane >= i * BLK, here, limit)
        tile = scores[j * BLK : (j + 1) * BLK] * (1.0 / math.sqrt(HD))
        tile = tile + (slant + slope * full(key_pos))
        tiles.append(jnp.where(ahead <= limit, tile, NEG_FILL))
    return jnp.concatenate(tiles)


def attend_body(heads, query_blocks, table, query, key, value, attended, level, value_t):
    @pl.when(pl.program_id(1) == 0)
    def turn():
        value_t[...] = half(full(value[...]).T)

    scores = score_rows(table, key[...], query[...], heads, query_blocks)
    top = jnp.max(scores, axis=0, keepdims=True)
    expon = jnp.exp(scores - top)
    total = jnp.sum(expon, axis=0, keepdims=True)
    probs = half(expon * (1.0 / total))
    attended[...] = half(dot(value_t[...], probs, 1, 0).T)
    level[...] = (top + jnp.log(total))[None]


def attend_back_body(
    heads,
    query_blocks,
    my_heads,
    split,
    table,
    query,
    key,
    value,
    level,
    *rest,
):
    rest, grad_parts = rest[len(PARTS) :], rest[: len(PARTS)]
    d_query, d_keys = (rest[0], rest[1]) if split else (rest[0], rest[0])
    grads, key_t, key_acc, value_acc = rest[-4:]
    head, block = pl.program_id(0), pl.program_id(1)
    rows = query.shape[0]
    scale = 1.0 / math.sqrt(HD)

    def columns(place):
        return pl.ds(pl.multiple_of((place * my_heads + head) * HD, HD), HD)

    @pl.when(block == 0)
    def begin():
        begin_row = 0
        for part in grad_parts:
            grads[begin_row : begin_row + part.shape[0], :] = part[...]
            begin_row += part.shape[0]
        key_t[...] = half(full(key[...]).T)
        key_acc[...] = jnp.zeros_like(key_acc)
        value_acc[...] = jnp.zeros_like(value_acc)

    scores = score_rows(table, key[...], query[...], heads, query_blocks)
    probs = jnp.exp(scores - level[0])
    grad = grads[pl.ds(pl.multiple_of(block * rows, rows), rows), :]
    d_probs = dot(value[...], grad, 1, 1)
    delta = jnp.sum(probs * d_probs, axis=0, keepdims=True)
    d_scores = half(probs * (d_probs - delta))
    turned = (dot(key_t[...], d_scores, 1, 0) * scale).T
    d_query[pl.ds(pl.multiple_of(block * rows, rows), rows), columns(0)] = half(turned)
    key_acc[...] += dot(d_scores, query[...], 1, 0)
    value_acc[...] += dot(half(probs), grad, 1, 0)

    @pl.when(block == pl.num_programs(1) - 1)
    def end():
        shift = 0 if split else 1
        d_keys[:, columns(shift)] = half(key_acc[...] * scale)
        d_keys[:, columns(shift + 1)] = half(value_acc[...])


def attention(table, heads, my_heads, query, keys, first, grad=None, level=None):
    rows, total = query.shape[0], keys.shape[0]
    step = 256 if total <= 1024 else BLK
    columns = my_heads * HD
    scalars = pl.BlockSpec(memory_space=pltpu.SMEM)
    of_query = pl.BlockSpec((step, HD), lambda h, i: (i, h))
    of_level = pl.BlockSpec((1, 1, step), lambda h, i: (h, 0, i))
    in_specs = [
        scalars,
        of_query,
        pl.BlockSpec((total, HD), lambda h, i: (0, first + h)),
        pl.BlockSpec((total, HD), lambda h, i: (0, first + my_heads + h)),
    ]
    common = {
        "grid": (my_heads, rows // step),
        "compiler_params": pltpu.CompilerParams(vmem_limit_bytes=48 << 20),
        "cost_estimate": pl.CostEstimate(
            flops=(4 if grad is None else 10) * rows * total * columns,
            bytes_accessed=32 << 20,
            transcendentals=my_heads * rows * total,
        ),
    }
    if grad is None:
        return pl.pallas_call(
            functools.partial(attend_body, heads, rows // BLK),
            in_specs=in_specs,
            out_specs=[of_query, of_level],
            out_shape=[
                jax.ShapeDtypeStruct((rows, columns), jnp.bfloat16),
                jax.ShapeDtypeStruct((my_heads, 1, rows), jnp.float32),
            ],
            scratch_shapes=[pltpu.VMEM((HD, total), jnp.bfloat16)],
            name="attend",
            **common,
        )(table, *in_hbm(query, keys, keys))
    split = query is not keys
    shapes = [(rows, columns), (total, 2 * columns)] if split else [(rows, 3 * columns)]
    return pl.pallas_call(
        functools.partial(attend_back_body, heads, rows // BLK, my_heads, split),
        in_specs=in_specs
        + [of_level]
        + [pl.BlockSpec((part.shape[0], HD), lambda h, i: (0, h)) for part in grad],
        out_specs=[pl.BlockSpec(shape, lambda h, i: (0, 0)) for shape in shapes],
        out_shape=[jax.ShapeDtypeStruct(shape, jnp.bfloat16) for shape in shapes],
        scratch_shapes=[
            pltpu.VMEM((rows, HD), jnp.bfloat16),
            pltpu.VMEM((HD, total), jnp.bfloat16),
            pltpu.VMEM((total, HD), jnp.float32),
            pltpu.VMEM((total, HD), jnp.float32),
        ],
        name="attend_back",
        **common,
    )(table, *in_hbm(query, keys, keys, level, *grad))


def products(parts, matrix, name):
    count, tile = len(parts), 512

    def body(*refs):
        for part, out in zip(refs[:count], refs[count + 1 :], strict=True):
            out[...] = dot(part[...], refs[count][...], 1, 1, jnp.bfloat16)

    return pl.pallas_call(
        body,
        grid=(matrix.shape[0] // tile,),
        in_specs=[pl.BlockSpec(v.shape, lambda i: (0, 0)) for v in parts]
        + [pl.BlockSpec((tile, matrix.shape[1]), lambda i: (i, 0))],
        out_specs=[pl.BlockSpec((v.shape[0], tile), lambda i: (0, i)) for v in parts],
        out_shape=[
            jax.ShapeDtypeStruct((v.shape[0], matrix.shape[0]), jnp.bfloat16) for v in parts
        ],
        **settings(name),
    )(*parts, matrix)


def gather_rows(rows):
    rows = lax.all_gather(rows, TOKENS, axis=1, tiled=True)
    return rows.reshape(-1, rows.shape[2])


def from_places(grad, groups, name):
    places, n, width = grad.shape
    part = width // groups

    def body(grad_ref, out_ref):
        for group in range(groups):
            for place in range(places):
                begin = (group * places + place) * part
                out_ref[:, begin : begin + part] = full(
                    grad_ref[place, :, group * part : (group + 1) * part]
                )

    return pl.pallas_call(
        body,
        out_shape=jax.ShapeDtypeStruct((n, places * width), jnp.float32),
        **settings(name),
    )(grad)


def norm_back(sums, rows, gain, direct, name, branch):
    n, width = rows.shape
    step = 32

    def body(part, upward, downward, rows_ref, gain_ref, direct_ref, grad_ref, *rest):
        @pl.when(pl.program_id(0) == 0)
        def begin():
            for ref in rest[-3 if branch else -2 :]:
                ref[...] = jnp.zeros_like(ref)

        grad = full(part[...]) + full(upward[...]) + full(downward[...])
        normed, scale = normalize(full(rows_ref[...]))
        out = full(direct_ref[...]) + normalize_back(normed, scale, grad * gain_ref[...])
        grad_ref[...] = out
        if branch:
            rounded = half(out)
            rest[0][...] = rounded
            rest[-3][...] += jnp.sum(full(rounded), axis=0, keepdims=True)
        rest[-2][...] += jnp.sum(grad * normed, axis=0, keepdims=True)
        rest[-1][...] += jnp.sum(grad, axis=0, keepdims=True)

    tile = pl.BlockSpec((step, width), lambda i: (i, 0))
    line = pl.BlockSpec((1, width), lambda i: (0, 0))
    lines = 3 if branch else 2
    return pl.pallas_call(
        body,
        grid=(n // step,),
        in_specs=[tile] * 4 + [line, tile],
        out_specs=[tile] * (2 if branch else 1) + [line] * lines,
        out_shape=[jax.ShapeDtypeStruct((n, width), jnp.float32)]
        + [jax.ShapeDtypeStruct((n, width), jnp.bfloat16)] * branch
        + [jax.ShapeDtypeStruct((1, width), jnp.float32)] * lines,
        **settings(name),
    )(*sums, rows, gain.reshape(1, -1), direct)


def converted(values, name):
    def body(values_ref, out_ref):
        out_ref[...] = full(values_ref[...])

    return pl.pallas_call(
        body, out_shape=jax.ShapeDtypeStruct(values.shape, jnp.float32), **settings(name)
    )(values)


def total(sums, rows, bias, name):
    def body(part, upward, downward, rows_ref, bias_ref, out_ref):
        out = full(part[...]) + full(upward[...]) + full(downward[...])
        out_ref[...] = half(rows_ref[...] + out + bias_ref[...])

    return pl.pallas_call(
        body, out_shape=jax.ShapeDtypeStruct(rows.shape, jnp.bfloat16), **settings(name)
    )(*sums, rows, bias.reshape(1, -1))


def rows_by_place(vectors, name):
    widths = [v.shape[1] // PLACES for v in vectors]

    def body(*refs):
        begin = 0
        for ref, width in zip(refs[:-1], widths, strict=True):
            for place in range(PLACES):
                refs[-1][place : place + 1, begin : begin + width] = ref[
                    :, place * width : (place + 1) * width
                ]
            begin += width

    return pl.pallas_call(
        body,
        out_shape=jax.ShapeDtypeStruct((PLACES, sum(widths)), jnp.float32),
        **settings(name),
    )(*vectors)


def with_rows(pieces, rows, name):
    places, n, width = pieces.shape
    more = -(-rows.shape[1] // width)
    padded = -(-more // 16) * 16

    def body(pieces_ref, rows_ref, out_ref):
        out_ref[:, :n, :] = pieces_ref[...]
        out_ref[:, n:, :] = jnp.zeros((places, padded, width), jnp.bfloat16)
        for place in range(places):
            lines = [
                rows_ref[place : place + 1, i * width : (i + 1) * width] for i in range(more)
            ]
            lines.append(jnp.zeros((padded - more, width), jnp.float32))
            out_ref[place, n:, :] = half(jnp.concatenate(lines))

    return pl.pallas_call(
        body,
        out_shape=jax.ShapeDtypeStruct((places, n + padded, width), jnp.bfloat16),
        **settings(name),
    )(pieces, rows)


def from_places_and_rows(received, groups, n, count, name):
    places, padded, width = received.shape
    part = width // groups
    more = count // width

    def body(received_ref, out_ref, sum_ref):
        for group in range(groups):
            for place in range(places):
                begin = (group * places + place) * part
                out_ref[:, begin : begin + part] = full(
                    received_ref[place, :n, group * part : (group + 1) * part]
                )
        lines = jnp.sum(full(received_ref[:, n:, :]), axis=0)
        for i in range(more):
            sum_ref[:, i * width : (i + 1) * width] = lines[i : i + 1]

    return pl.pallas_call(
        body,
        out_shape=[
            jax.ShapeDtypeStruct((n, places * width), jnp.float32),
            jax.ShapeDtypeStruct((1, count), jnp.float32),
        ],
        **settings(name),
    )(received)


def norm_sums(grads, rows, mixed, name):
    width, count, step = rows[0].shape[1], len(rows), 64
    columns = mixed[0].shape[1]

    def body(*refs):
        gain = jnp.zeros((1, width), jnp.float32)
        bias = jnp.zeros((1, width), jnp.float32)
        for grad_ref, rows_ref in zip(refs[:count], refs[count : 2 * count], strict=True):

            def add(i, carried, grad_ref=grad_ref, rows_ref=rows_ref):
                here = pl.ds(pl.multiple_of(i * step, step), step)
                grad = full(grad_ref[here, :])
                normed = normalize(full(rows_ref[here, :]))[0]
                return (
                    carried[0] + jnp.sum(grad * normed, axis=0, keepdims=True),
                    carried[1] + jnp.sum(grad, axis=0, keepdims=True),
                )

            gain, bias = lax.fori_loop(0, rows_ref.shape[0] // step, add, (gain, bias))
        refs[-3][...] = gain
        refs[-2][...] = bias
        refs[-1][...] = sum(
            jnp.sum(full(ref[...]), axis=0, keepdims=True) for ref in refs[2 * count : 3 * count]
        )

    return pl.pallas_call(
        body,
        out_shape=[jax.ShapeDtypeStruct((1, width), jnp.float32)] * 2
        + [jax.ShapeDtypeStruct((1, columns), jnp.float32)],
        **settings(name),
    )(*grads, *rows, *mixed)


def on_device(
    tokens,
    ln1_gain,
    ln1_bias,
    w_qkv,
    b_qv,
    w_out,
    b_out,
    ln2_gain,
    ln2_bias,
    w_in,
    b_in,
    w_down,
    b_down,
    cotangent,
    block_seg,
    block_pos,
):
    sp = lax.axis_size("sp")
    fs = lax.axis_size("fs")
    devices = PLACES * sp * fs
    my_tp = lax.axis_index("tp")
    my_sp = lax.axis_index("sp")
    local_rows, width = tokens.shape[1:]
    heads = width // HD
    my_heads = heads // PLACES
    head_cols = my_heads * HD
    hidden = w_in.shape[1] // PLACES
    group_rows = PLACES * local_rows

    def buffer(columns):
        return jnp.zeros((group_rows, columns), jnp.bfloat16)

    def by_part(rows):
        return [rows[a * local_rows : b * local_rows] for a, b in PARTS]

    order = [[SNAKE[(SNAKE.index(i) + s) % PLACES] for s in SHIFTS] for i in range(PLACES)]
    sources = jnp.asarray(order, jnp.int32)[my_tp]
    picked = (sources[:, None] == jnp.arange(PLACES, dtype=jnp.int32)[None, :]).astype(jnp.int32)

    def in_order(blocks):
        blocks = jnp.sum(picked[:, :, None, None] * blocks.reshape(1, PLACES, sp, -1), axis=1)
        mine = lax.dynamic_index_in_dim(blocks, my_sp, 1, keepdims=False).reshape(-1)
        return mine, blocks.transpose(1, 0, 2).reshape(-1)

    query_seg, key_seg = in_order(block_seg[0])
    query_pos, key_pos = in_order(block_pos[0])
    first_head = jnp.full((1,), my_tp * my_heads, jnp.int32)
    table = jnp.concatenate([query_pos, query_seg, key_pos, key_seg, first_head])

    small = [ln1_gain, ln1_bias, b_out, ln2_gain, ln2_bias, b_down, b_qv, b_in]
    sizes = [v.shape[0] for v in small]
    cuts = [sum(sizes[:i]) for i in range(len(sizes) + 1)]
    own, own_cot = tokens[0], cotangent[0]

    low1, high1 = hop(own, own)
    down_slice = lax.all_gather(half(w_down), TOKENS, axis=0, tiled=True)
    small_own, qkv_pieces = fence(half(jnp.concatenate(small)), by_place(w_qkv, 3))
    qkv_pieces = exchange(qkv_pieces)
    gathered = gather_small(small_own[None], bits_of(EVERY))
    low2, high2 = hop(low1, high1)
    in_pieces = by_place(w_in, 1)
    (
        low1,
        high1,
        low2,
        high2,
        qkv_pieces,
        in_pieces,
        gathered,
        down_slice,
        w_out,
        own_cot,
    ) = fence(
        low1,
        high1,
        low2,
        high2,
        qkv_pieces,
        in_pieces,
        gathered,
        down_slice,
        w_out,
        own_cot,
    )
    gathered = full(gathered)
    gain1, bias1, out_bias, gain2, bias2, down_bias, qv_bias, in_bias = (
        gathered[:, cuts[i] : cuts[i + 1]].reshape(-1) for i in range(len(sizes))
    )
    qv_bias = lax.dynamic_slice_in_dim(qv_bias.reshape(2, width), my_tp * head_cols, head_cols, 1)
    in_bias = lax.dynamic_slice_in_dim(in_bias, my_tp * hidden, hidden)

    def norm1(rows):
        return half(normalize(full(rows))[0] * gain1 + bias1)

    in_pieces = exchange(in_pieces)
    qkv_slice = gather_rows(qkv_pieces)
    out_slice = lax.all_gather(half(w_out), TOKENS, axis=0, tiled=True)
    token_parts = [own, join((low1, high1)), join((low2, high2))]
    low3, high3 = hop(low2, high2)
    normed = [norm1(part) for part in token_parts]
    low3, high3, own_cot, *normed = fence(low3, high3, own_cot, *normed)
    low4, high4 = last_hop(low3, high3)
    token_parts.append(join((low3, high3)))
    normed.append(norm1(token_parts[3]))
    blank = jnp.zeros((head_cols,), jnp.float32)
    qkv_bias = jnp.concatenate([qv_bias[0], blank, qv_bias[1]])
    mixed = [half(dot(part, qkv_slice, 1, 0) + qkv_bias) for part in normed]
    low4, high4, own_cot, qkv_slice, *mixed = fence(low4, high4, own_cot, qkv_slice, *mixed)

    cot_low1, cot_high1 = hop(own_cot, own_cot)
    token_parts.append(join((low4, high4)))
    normed.append(norm1(token_parts[4]))
    mixed = jnp.concatenate([*mixed, half(dot(normed[4], qkv_slice, 1, 0) + qkv_bias)])
    mixed, cot_low1, cot_high1, in_pieces, out_slice = fence(
        mixed, cot_low1, cot_high1, in_pieces, out_slice
    )
    in_slice = gather_rows(in_pieces)
    cot_low2, cot_high2 = hop(cot_low1, cot_high1)
    keys = mixed
    if sp > 1:
        keys = lax.all_gather(mixed[:, head_cols:], "sp", axis=0, tiled=True)
    first_key = my_heads if sp == 1 else 0
    attended, level = attention(table, heads, my_heads, mixed, keys, first_key)
    attended, cot_low2, cot_high2 = fence(attended, cot_low2, cot_high2)

    attended_parts = by_part(attended)
    branch_parts = [dot(attended_parts[i], out_slice, 1, 0, jnp.bfloat16) for i in range(5)]
    branch_low, branch_high = hop(*jnp.split(branch_parts[4], 2))
    cot_low3, cot_high3 = hop(cot_low2, cot_high2)
    branch_low, branch_high, cot_low3, cot_high3, *branch_parts = fence(
        branch_low, branch_high, cot_low3, cot_high3, *branch_parts
    )
    up, down = hop(*first_sum(branch_parts[3], branch_low, branch_high))
    cot_low4, cot_high4 = last_hop(cot_low3, cot_high3)
    up, down, cot_low4, cot_high4, in_slice = fence(up, down, cot_low4, cot_high4, in_slice)
    up, down = hop(*next_sum(branch_parts[2], up, down))
    cot_parts = [own_cot, join((cot_low1, cot_high1)), join((cot_low2, cot_high2))]
    cot_parts += [join((cot_low3, cot_high3)), join((cot_low4, cot_high4))]
    up, down, *cot_parts = fence(up, down, *cot_parts)
    up, down = fence(*hop(*next_sum(branch_parts[1], up, down)))
    residual = full(own) + last_sum(branch_parts[0], up, down) + out_bias

    own_normed2, scale2 = normalize(residual)
    second = half(own_normed2 * gain2 + bias2)
    second_parts, act_parts, d_pre_parts, d_second_parts, ffn_parts = [second], [], [], [], []
    low, high = second, second
    for index in range(5):
        if index < 3:
            new_low, new_high = hop(low, high)
        elif index == 3:
            new_low, new_high = last_hop(low, high)
        if index:
            second_parts.append(join((low, high)))
        pre_act = dot(second_parts[index], in_slice, 1, 0) + in_bias
        act, gelu_back = jax.vjp(lambda v: jax.nn.gelu(v, approximate=True), pre_act)
        act_parts.append(half(act))
        d_pre = half(gelu_back(dot(cot_parts[index], down_slice, 1, 1))[0])
        d_pre_parts.append(d_pre)
        d_second_parts.append(dot(d_pre, in_slice, 1, 1, jnp.bfloat16))
        made = [act_parts, d_pre_parts, d_second_parts]
        if index < 3:
            ffn_parts.append(dot(act_parts[index], down_slice, 1, 0, jnp.bfloat16))
            made.append(ffn_parts)
        if index < 4:
            low, high, *held = fence(new_low, new_high, *[parts[index] for parts in made])
            for parts, value in zip(made, held, strict=True):
                parts[index] = value

    low, high = hop(*jnp.split(d_second_parts[4], 2))
    ffn_parts += [dot(act, down_slice, 1, 0, jnp.bfloat16) for act in act_parts[3:]]
    low, high, d_pre_parts[4], act_parts[4], *ffn_parts = fence(
        low, high, d_pre_parts[4], act_parts[4], *ffn_parts
    )
    up, down = hop(*first_sum(d_second_parts[3], low, high))
    out_up, out_down = hop(*jnp.split(ffn_parts[4], 2))
    grad_in = rows_product(second_parts, d_pre_parts, 512, "grad_in")
    grad_in = grad_in.reshape(PLACES, -1, hidden)
    up, down, out_up, out_down, grad_in = fence(up, down, out_up, out_down, grad_in)
    grad_in = lax.psum_scatter(grad_in, TOKENS, scatter_dimension=1, tiled=True)
    up, down = hop(*next_sum(d_second_parts[2], up, down))
    out_up, out_down = hop(*first_sum(ffn_parts[3], out_up, out_down))
    up, down, out_up, out_down, act_parts[4] = fence(up, down, out_up, out_down, act_parts[4])
    up, down = hop(*next_sum(d_second_parts[1], up, down))
    out_up, out_down = hop(*next_sum(ffn_parts[2], out_up, out_down))
    grad_down = rows_product(act_parts, cot_parts, 256, "grad_down")
    grad_b_in = sum(jnp.sum(full(part), axis=0) for part in d_pre_parts)
    blank = jnp.zeros((PLACES * hidden,), jnp.float32)
    grad_b_in = lax.dynamic_update_slice_in_dim(blank, grad_b_in, my_tp * hidden, 0)
    g_b_down = jnp.sum(full(own_cot), axis=0)
    up, down, out_up, out_down, grad_down, grad_b_in = fence(
        up, down, out_up, out_down, grad_down, grad_b_in
    )
    grad_down = lax.psum_scatter(grad_down, TOKENS, scatter_dimension=0, tiled=True)

    d_residual, d_branch, g_b_out, g_gain2, g_bias2 = norm_back(
        (d_second_parts[0], up, down), residual, gain2, own_cot, "norm2_back", True
    )
    low, high = hop(d_branch, d_branch)
    out_up, out_down = hop(*next_sum(ffn_parts[1], out_up, out_down))
    low, high, out_up, out_down = fence(low, high, out_up, out_down)
    d_branch_parts, d_attended = [d_branch], [dot(d_branch, out_slice, 1, 1, jnp.bfloat16)]
    for index in range(1, 5):
        d_branch_parts.append(join((low, high)))
        d_attended.append(dot(d_branch_parts[index], out_slice, 1, 1, jnp.bfloat16))
        if index < 3:
            low, high = hop(low, high)
            low, high, grad_in, d_attended[index] = fence(low, high, grad_in, d_attended[index])
        elif index == 3:
            low, high = last_hop(low, high)
            low, high, grad_in, d_attended[index] = fence(low, high, grad_in, d_attended[index])
            grad_in = exchange(grad_in)

    grads = attention(table, heads, my_heads, mixed, keys, first_key, d_attended, level)
    if sp == 1:
        (d_mixed,) = grads
    else:
        d_keys = half(lax.psum_scatter(full(grads[1]), "sp", scatter_dimension=0, tiled=True))
        d_mixed = jnp.concatenate([grads[0], d_keys], axis=1)
    d_mixed, d_branch_parts[4], grad_down = fence(d_mixed, d_branch_parts[4], grad_down)

    mixed_parts = by_part(d_mixed)
    far = dot(mixed_parts[4], qkv_slice, 1, 1, jnp.bfloat16)
    low, high = hop(*jnp.split(far, 2))
    (near,) = products(mixed_parts[3:4], qkv_slice, "d_normed_near")
    grad_qkv = rows_product(normed, mixed_parts, 512, "grad_qkv")
    grad_qkv = grad_qkv.reshape(PLACES, -1, 3 * head_cols)
    low, high, near, grad_qkv, mixed_parts[0] = fence(low, high, near, grad_qkv, mixed_parts[0])
    grad_qkv = lax.psum_scatter(grad_qkv, TOKENS, scatter_dimension=1, tiled=True)
    up, down = hop(*first_sum(near, low, high))
    d_normed = [*products(mixed_parts[:3], qkv_slice, "d_normed"), near, far]
    g_gain1, g_bias1, mixed_sum = norm_sums(d_normed, token_parts, mixed_parts, "norm1_sums")
    up, down, grad_in, g_gain1, g_bias1, mixed_sum, *d_normed[:3] = fence(
        up, down, grad_in, g_gain1, g_bias1, mixed_sum, *d_normed[:3]
    )
    up, down = hop(*next_sum(d_normed[2], up, down))
    grad_out = rows_product(attended_parts, d_branch_parts, 128, "grad_out")
    grad_w_in = from_places(grad_in, 1, "in_back")
    grad_b_qv = jnp.zeros((2, width), jnp.float32)
    for i in range(2):
        piece = mixed_sum[:, 2 * i * head_cols : (2 * i + 1) * head_cols]
        grad_b_qv = lax.dynamic_update_slice(grad_b_qv, piece, (i, my_tp * head_cols))
    whole = [g_gain1, g_bias1, g_b_out, g_gain2, g_bias2, g_b_down, grad_b_qv, grad_b_in]
    summed = rows_by_place([v.reshape(1, -1) for v in whole], "sums_by_place")
    summed = sum_small(summed, TOKENS)
    own_rows = grad_qkv.shape[1]
    grad_qkv = with_rows(grad_qkv, summed, "qkv_with_sums")
    up, down, grad_out, grad_w_in, grad_qkv = fence(up, down, grad_out, grad_w_in, grad_qkv)
    up, down = hop(*next_sum(d_normed[1], up, down))
    grad_qkv = exchange(grad_qkv)
    grad_w_down = converted(grad_down, "down_back")
    output = total((ffn_parts[0], out_up, out_down), residual, down_bias, "output")
    up, down, grad_w_down, output, grad_qkv = fence(up, down, grad_w_down, output, grad_qkv)
    grad_out = lax.psum_scatter(grad_out, TOKENS, scatter_dimension=0, tiled=True)
    grad_tokens = norm_back((d_normed[0], up, down), own, gain1, d_residual, "norm1_back", False)[0]
    grad_w_out = converted(grad_out, "out_back")
    grad_w_qkv, summed = from_places_and_rows(
        grad_qkv, 3, own_rows, summed.shape[1], "qkv_back"
    )
    near_devices = sp * fs
    place = my_sp * fs + lax.axis_index("fs")
    g_gain1, g_bias1, g_b_out, g_gain2, g_bias2, g_b_down, g_b_qv, g_b_in = (
        lax.dynamic_slice_in_dim(summed, cuts[i] * near_devices + place * sizes[i], sizes[i], 1)[0]
        for i in range(len(sizes))
    )
    return (
        output[None],
        grad_tokens[None],
        g_gain1,
        g_bias1,
        grad_w_qkv,
        g_b_qv,
        grad_w_out,
        g_b_out,
        g_gain2,
        g_bias2,
        grad_w_in,
        g_b_in,
        grad_w_down,
        g_b_down,
    )


def solution(mesh):
    ctx, fs = mesh.shape["ctx"], mesh.shape["fsdp"]
    inner = Mesh(mesh.devices.reshape(PLACES, ctx // PLACES, fs), EVERY)
    rows = P("fs", ("tp", "sp"), None)
    vector, matrix, blocks = P(EVERY), P(EVERY, None), P("fs", None)
    kinds = (
        rows,
        vector,
        vector,
        matrix,
        vector,
        matrix,
        vector,
        vector,
        vector,
        matrix,
        vector,
        matrix,
        vector,
    )
    return jax.shard_map(
        on_device,
        mesh=inner,
        in_specs=kinds + (rows, blocks, blocks),
        out_specs=(rows,) + kinds,
        check_vma=False,
    )
```

```python
import functools
import math

import jax
import jax.numpy as jnp
from jax import lax
from jax.experimental import pallas as pl
from jax.experimental.pallas import tpu as pltpu
from jax.sharding import Mesh
from jax.sharding import PartitionSpec as P

HD = 128
BLK = 128
EPSILON = 1e-05
NEG_FILL = -1e30

EVERY = ("tp", "sp", "fs")
TOKENS = ("sp", "fs")
SNAKE = (0, 2, 4, 6, 7, 5, 3, 1)
PLACES = len(SNAKE)
SHIFTS = (0, -1, 1, -2, 2, -3, 3, 4)
PARTS = ((0, 1), (1, 3), (3, 5), (5, 7), (7, 8))


def half(values):
    return values.astype(jnp.bfloat16)


def full(values):
    return values.astype(jnp.float32)


def dot(left, right, left_dim, right_dim, out=jnp.float32):
    return lax.dot_general(
        left, right, (((left_dim,), (right_dim,)), ((), ())), preferred_element_type=jnp.float32
    ).astype(out)


def fence(*values):
    return lax.optimization_barrier(values)


def normalize(values):
    center = values - jnp.mean(values, axis=-1, keepdims=True)
    spread = jnp.mean(center * center, axis=-1, keepdims=True)
    scale = lax.rsqrt(spread + EPSILON)
    return center * scale, scale


def normalize_back(normed, scale, grad):
    return scale * (
        grad
        - jnp.mean(grad, axis=-1, keepdims=True)
        - normed * jnp.mean(grad * normed, axis=-1, keepdims=True)
    )


def hop(upward, downward):
    up = [(SNAKE[i], SNAKE[(i + 1) % PLACES]) for i in range(PLACES)]
    down = [(b, a) for a, b in up]
    return lax.ppermute(upward, "tp", up), lax.ppermute(downward, "tp", down)


def last_hop(below, above):
    n = below.shape[0] // 2
    return hop(below[:n], above[n:])


def first_sum(part, low, high):
    below, above = jnp.split(part, 2)
    n = below.shape[0] // 2
    upward = jnp.concatenate([half(full(above[:n]) + full(low)), above[n:]])
    downward = jnp.concatenate([below[:n], half(full(below[n:]) + full(high))])
    return upward, downward


def next_sum(part, upward, downward):
    below, above = jnp.split(part, 2)
    return half(full(above) + full(upward)), half(full(below) + full(downward))


def last_sum(part, upward, downward):
    return full(part) + full(upward) + full(downward)


def join(pair):
    return jnp.concatenate(pair)


def put(buffer, part, index, local_rows):
    return lax.dynamic_update_slice_in_dim(buffer, part, PARTS[index][0] * local_rows, 0)


def bits_of(names):
    return [
        (name, 1 << bit, lax.axis_size(name))
        for name in reversed(names)
        for bit in range(lax.axis_size(name).bit_length() - 1)
    ]


def swap(values, name, bit, size):
    return lax.ppermute(values, name, [(i, i ^ bit) for i in range(size)])


def gather_small(values, bits):
    for name, bit, size in bits:
        other = swap(values, name, bit, size)
        first = (lax.axis_index(name) & bit) == 0
        values = jnp.concatenate([jnp.where(first, values, other), jnp.where(first, other, values)])
    return values


def sum_small(values, names):
    for name, bit, size in bits_of(names):
        values = values + swap(values, name, bit, size)
    return values


def by_place(rows, groups):
    n, width = rows.shape
    part = width // groups // PLACES
    rows = half(rows).reshape(n, groups, PLACES, part).transpose(2, 0, 1, 3)
    return rows.reshape(PLACES, n, groups * part)


def exchange(pieces):
    return lax.all_to_all(pieces, "tp", split_axis=0, concat_axis=0, tiled=True)


def in_hbm(*arrays):
    return [pltpu.with_memory_space_constraint(v, pltpu.HBM) for v in arrays]


def settings(name, megabytes=40):
    return {
        "compiler_params": pltpu.CompilerParams(vmem_limit_bytes=megabytes << 20),
        "cost_estimate": pl.CostEstimate(flops=1 << 20, bytes_accessed=1 << 20, transcendentals=0),
        "name": name,
    }


def rows_product(lefts, rights, tile, name):
    count, out_rows, out_cols = len(lefts), lefts[0].shape[1], rights[0].shape[1]

    def body(*refs):
        total = None
        for left, right in zip(refs[:count], refs[count : 2 * count], strict=True):
            term = lax.dot_general(
                left[...],
                right[...],
                (((0,), (0,)), ((), ())),
                preferred_element_type=jnp.float32,
            )
            total = term if total is None else total + term
        refs[2 * count][...] = half(total)

    return pl.pallas_call(
        body,
        grid=(out_rows // tile,),
        in_specs=[pl.BlockSpec((v.shape[0], tile), lambda i: (0, i)) for v in lefts]
        + [pl.BlockSpec(v.shape, lambda i: (0, 0)) for v in rights],
        out_specs=pl.BlockSpec((tile, out_cols), lambda i: (i, 0)),
        out_shape=pltpu.HBM((out_rows, out_cols), jnp.bfloat16),
        **settings(name),
    )(*lefts, *rights)


def score_rows(table, keys, queries, heads, query_blocks):
    scores = dot(keys, queries, 1, 1)
    count, key_blocks = queries.shape[0] // BLK, keys.shape[0] // BLK
    lane = lax.broadcasted_iota(jnp.int32, (1, queries.shape[0]), 1)
    down = lax.broadcasted_iota(jnp.int32, (BLK, queries.shape[0]), 0)
    ahead = down - lax.rem(lane, BLK)
    head = table[2 * query_blocks + 2 * key_blocks] + pl.program_id(0)
    slope = jnp.exp2(full(jnp.full(down.shape, head + 1, jnp.int32)) * (-8.0 / heads))
    slant = slope * full(down)
    tiles = []
    for j in range(key_blocks):
        key_pos = table[2 * query_blocks + j]
        key_seg = table[2 * query_blocks + key_blocks + j]
        limit = jnp.zeros((1, queries.shape[0]), jnp.int32)
        for i in range(count):
            block = pl.program_id(1) * count + i
            seen = (key_seg == 0) | (key_seg == table[query_blocks + block])
            here = jnp.where(seen, table[block] - key_pos, -BLK)
            limit = jnp.where(lane >= i * BLK, here, limit)
        tile = scores[j * BLK : (j + 1) * BLK] * (1.0 / math.sqrt(HD))
        tile = tile + (slant + slope * full(key_pos))
        tiles.append(jnp.where(ahead <= limit, tile, NEG_FILL))
    return jnp.concatenate(tiles)


def attend_body(heads, query_blocks, table, query, key, value, attended, level, value_t):
    @pl.when(pl.program_id(1) == 0)
    def turn():
        value_t[...] = half(full(value[...]).T)

    scores = score_rows(table, key[...], query[...], heads, query_blocks)
    top = jnp.max(scores, axis=0, keepdims=True)
    expon = jnp.exp(scores - top)
    total = jnp.sum(expon, axis=0, keepdims=True)
    probs = half(expon * (1.0 / total))
    attended[...] = half(dot(value_t[...], probs, 1, 0).T)
    level[...] = (top + jnp.log(total))[None]


def attend_back_body(
    heads,
    query_blocks,
    my_heads,
    split,
    table,
    query,
    key,
    value,
    level,
    *rest,
):
    rest, grad_parts = rest[len(PARTS) :], rest[: len(PARTS)]
    d_query, d_keys = (rest[0], rest[1]) if split else (rest[0], rest[0])
    grads, key_t, key_acc, value_acc = rest[-4:]
    head, block = pl.program_id(0), pl.program_id(1)
    rows = query.shape[0]
    scale = 1.0 / math.sqrt(HD)

    def columns(place):
        return pl.ds(pl.multiple_of((place * my_heads + head) * HD, HD), HD)

    @pl.when(block == 0)
    def begin():
        begin_row = 0
        for part in grad_parts:
            grads[begin_row : begin_row + part.shape[0], :] = part[...]
            begin_row += part.shape[0]
        key_t[...] = half(full(key[...]).T)
        key_acc[...] = jnp.zeros_like(key_acc)
        value_acc[...] = jnp.zeros_like(value_acc)

    scores = score_rows(table, key[...], query[...], heads, query_blocks)
    probs = jnp.exp(scores - level[0])
    grad = grads[pl.ds(pl.multiple_of(block * rows, rows), rows), :]
    d_probs = dot(value[...], grad, 1, 1)
    delta = jnp.sum(probs * d_probs, axis=0, keepdims=True)
    d_scores = half(probs * (d_probs - delta))
    turned = (dot(key_t[...], d_scores, 1, 0) * scale).T
    d_query[pl.ds(pl.multiple_of(block * rows, rows), rows), columns(0)] = half(turned)
    key_acc[...] += dot(d_scores, query[...], 1, 0)
    value_acc[...] += dot(half(probs), grad, 1, 0)

    @pl.when(block == pl.num_programs(1) - 1)
    def end():
        shift = 0 if split else 1
        d_keys[:, columns(shift)] = half(key_acc[...] * scale)
        d_keys[:, columns(shift + 1)] = half(value_acc[...])


def attention(table, heads, my_heads, query, keys, first, grad=None, level=None):
    rows, total = query.shape[0], keys.shape[0]
    step = 256 if total <= 1024 else BLK
    columns = my_heads * HD
    scalars = pl.BlockSpec(memory_space=pltpu.SMEM)
    of_query = pl.BlockSpec((step, HD), lambda h, i: (i, h))
    of_level = pl.BlockSpec((1, 1, step), lambda h, i: (h, 0, i))
    in_specs = [
        scalars,
        of_query,
        pl.BlockSpec((total, HD), lambda h, i: (0, first + h)),
        pl.BlockSpec((total, HD), lambda h, i: (0, first + my_heads + h)),
    ]
    common = {
        "grid": (my_heads, rows // step),
        "compiler_params": pltpu.CompilerParams(vmem_limit_bytes=48 << 20),
        "cost_estimate": pl.CostEstimate(
            flops=(4 if grad is None else 10) * rows * total * columns,
            bytes_accessed=32 << 20,
            transcendentals=my_heads * rows * total,
        ),
    }
    if grad is None:
        return pl.pallas_call(
            functools.partial(attend_body, heads, rows // BLK),
            in_specs=in_specs,
            out_specs=[of_query, of_level],
            out_shape=[
                jax.ShapeDtypeStruct((rows, columns), jnp.bfloat16),
                jax.ShapeDtypeStruct((my_heads, 1, rows), jnp.float32),
            ],
            scratch_shapes=[pltpu.VMEM((HD, total), jnp.bfloat16)],
            name="attend",
            **common,
        )(table, *in_hbm(query, keys, keys))
    split = query is not keys
    shapes = [(rows, columns), (total, 2 * columns)] if split else [(rows, 3 * columns)]
    return pl.pallas_call(
        functools.partial(attend_back_body, heads, rows // BLK, my_heads, split),
        in_specs=in_specs
        + [of_level]
        + [pl.BlockSpec((part.shape[0], HD), lambda h, i: (0, h)) for part in grad],
        out_specs=[pl.BlockSpec(shape, lambda h, i: (0, 0)) for shape in shapes],
        out_shape=[jax.ShapeDtypeStruct(shape, jnp.bfloat16) for shape in shapes],
        scratch_shapes=[
            pltpu.VMEM((rows, HD), jnp.bfloat16),
            pltpu.VMEM((HD, total), jnp.bfloat16),
            pltpu.VMEM((total, HD), jnp.float32),
            pltpu.VMEM((total, HD), jnp.float32),
        ],
        name="attend_back",
        **common,
    )(table, *in_hbm(query, keys, keys, level, *grad))


def products(parts, matrix, name):
    count, tile = len(parts), 512

    def body(*refs):
        for part, out in zip(refs[:count], refs[count + 1 :], strict=True):
            out[...] = dot(part[...], refs[count][...], 1, 1, jnp.bfloat16)

    return pl.pallas_call(
        body,
        grid=(matrix.shape[0] // tile,),
        in_specs=[pl.BlockSpec(v.shape, lambda i: (0, 0)) for v in parts]
        + [pl.BlockSpec((tile, matrix.shape[1]), lambda i: (i, 0))],
        out_specs=[pl.BlockSpec((v.shape[0], tile), lambda i: (0, i)) for v in parts],
        out_shape=[
            jax.ShapeDtypeStruct((v.shape[0], matrix.shape[0]), jnp.bfloat16) for v in parts
        ],
        **settings(name),
    )(*parts, matrix)


def gather_rows(rows):
    rows = lax.all_gather(rows, TOKENS, axis=1, tiled=True)
    return rows.reshape(-1, rows.shape[2])


def from_places(grad, groups, name):
    places, n, width = grad.shape
    part = width // groups

    def body(grad_ref, out_ref):
        for group in range(groups):
            for place in range(places):
                begin = (group * places + place) * part
                out_ref[:, begin : begin + part] = full(
                    grad_ref[place, :, group * part : (group + 1) * part]
                )

    return pl.pallas_call(
        body,
        out_shape=jax.ShapeDtypeStruct((n, places * width), jnp.float32),
        **settings(name),
    )(grad)


def norm_back(sums, rows, gain, direct, name, branch):
    n, width = rows.shape
    step = 64

    def body(part, upward, downward, rows_ref, gain_ref, direct_ref, grad_ref, *rest):
        @pl.when(pl.program_id(0) == 0)
        def begin():
            for ref in rest[-3 if branch else -2 :]:
                ref[...] = jnp.zeros_like(ref)

        grad = full(part[...]) + full(upward[...]) + full(downward[...])
        normed, scale = normalize(full(rows_ref[...]))
        out = full(direct_ref[...]) + normalize_back(normed, scale, grad * gain_ref[...])
        grad_ref[...] = out
        if branch:
            rounded = half(out)
            rest[0][...] = rounded
            rest[-3][...] += jnp.sum(full(rounded), axis=0, keepdims=True)
        rest[-2][...] += jnp.sum(grad * normed, axis=0, keepdims=True)
        rest[-1][...] += jnp.sum(grad, axis=0, keepdims=True)

    tile = pl.BlockSpec((step, width), lambda i: (i, 0))
    line = pl.BlockSpec((1, width), lambda i: (0, 0))
    lines = 3 if branch else 2
    return pl.pallas_call(
        body,
        grid=(n // step,),
        in_specs=[tile] * 4 + [line, tile],
        out_specs=[tile] * (2 if branch else 1) + [line] * lines,
        out_shape=[jax.ShapeDtypeStruct((n, width), jnp.float32)]
        + [jax.ShapeDtypeStruct((n, width), jnp.bfloat16)] * branch
        + [jax.ShapeDtypeStruct((1, width), jnp.float32)] * lines,
        **settings(name),
    )(*sums, rows, gain.reshape(1, -1), direct)


def converted(values, name):
    def body(values_ref, out_ref):
        out_ref[...] = full(values_ref[...])

    return pl.pallas_call(
        body, out_shape=jax.ShapeDtypeStruct(values.shape, jnp.float32), **settings(name)
    )(values)


def total(sums, rows, bias, name):
    def body(part, upward, downward, rows_ref, bias_ref, out_ref):
        out = full(part[...]) + full(upward[...]) + full(downward[...])
        out_ref[...] = half(rows_ref[...] + out + bias_ref[...])

    return pl.pallas_call(
        body, out_shape=jax.ShapeDtypeStruct(rows.shape, jnp.bfloat16), **settings(name)
    )(*sums, rows, bias.reshape(1, -1))


def rows_by_place(vectors, name):
    widths = [v.shape[1] // PLACES for v in vectors]

    def body(*refs):
        begin = 0
        for ref, width in zip(refs[:-1], widths, strict=True):
            for place in range(PLACES):
                refs[-1][place : place + 1, begin : begin + width] = ref[
                    :, place * width : (place + 1) * width
                ]
            begin += width

    return pl.pallas_call(
        body,
        out_shape=jax.ShapeDtypeStruct((PLACES, sum(widths)), jnp.float32),
        **settings(name),
    )(*vectors)


def with_rows(pieces, rows, name):
    places, n, width = pieces.shape
    more = -(-rows.shape[1] // width)
    padded = -(-more // 8) * 8

    def body(pieces_ref, rows_ref, out_ref):
        out_ref[:, :n, :] = pieces_ref[...]
        out_ref[:, n:, :] = jnp.zeros((places, padded, width), jnp.bfloat16)
        for place in range(places):
            lines = [
                rows_ref[place : place + 1, i * width : (i + 1) * width] for i in range(more)
            ]
            lines.append(jnp.zeros((padded - more, width), jnp.float32))
            out_ref[place, n:, :] = half(jnp.concatenate(lines))

    return pl.pallas_call(
        body,
        out_shape=jax.ShapeDtypeStruct((places, n + padded, width), jnp.bfloat16),
        **settings(name),
    )(pieces, rows)


def from_places_and_rows(received, groups, n, count, name):
    places, padded, width = received.shape
    part = width // groups
    more = count // width

    def body(received_ref, out_ref, sum_ref):
        for group in range(groups):
            for place in range(places):
                begin = (group * places + place) * part
                out_ref[:, begin : begin + part] = full(
                    received_ref[place, :n, group * part : (group + 1) * part]
                )
        lines = jnp.sum(full(received_ref[:, n:, :]), axis=0)
        for i in range(more):
            sum_ref[:, i * width : (i + 1) * width] = lines[i : i + 1]

    return pl.pallas_call(
        body,
        out_shape=[
            jax.ShapeDtypeStruct((n, places * width), jnp.float32),
            jax.ShapeDtypeStruct((1, count), jnp.float32),
        ],
        **settings(name),
    )(received)


def norm_sums(grads, rows, mixed, name):
    width, count, step = rows[0].shape[1], len(rows), 64
    columns = mixed[0].shape[1]

    def body(*refs):
        gain = jnp.zeros((1, width), jnp.float32)
        bias = jnp.zeros((1, width), jnp.float32)
        for grad_ref, rows_ref in zip(refs[:count], refs[count : 2 * count], strict=True):

            def add(i, carried, grad_ref=grad_ref, rows_ref=rows_ref):
                here = pl.ds(pl.multiple_of(i * step, step), step)
                grad = full(grad_ref[here, :])
                normed = normalize(full(rows_ref[here, :]))[0]
                return (
                    carried[0] + jnp.sum(grad * normed, axis=0, keepdims=True),
                    carried[1] + jnp.sum(grad, axis=0, keepdims=True),
                )

            gain, bias = lax.fori_loop(0, rows_ref.shape[0] // step, add, (gain, bias))
        refs[-3][...] = gain
        refs[-2][...] = bias
        refs[-1][...] = sum(
            jnp.sum(full(ref[...]), axis=0, keepdims=True) for ref in refs[2 * count : 3 * count]
        )

    return pl.pallas_call(
        body,
        out_shape=[jax.ShapeDtypeStruct((1, width), jnp.float32)] * 2
        + [jax.ShapeDtypeStruct((1, columns), jnp.float32)],
        **settings(name),
    )(*grads, *rows, *mixed)


def on_device(
    tokens,
    ln1_gain,
    ln1_bias,
    w_qkv,
    b_qv,
    w_out,
    b_out,
    ln2_gain,
    ln2_bias,
    w_in,
    b_in,
    w_down,
    b_down,
    cotangent,
    block_seg,
    block_pos,
):
    sp = lax.axis_size("sp")
    fs = lax.axis_size("fs")
    devices = PLACES * sp * fs
    my_tp = lax.axis_index("tp")
    my_sp = lax.axis_index("sp")
    local_rows, width = tokens.shape[1:]
    heads = width // HD
    my_heads = heads // PLACES
    head_cols = my_heads * HD
    hidden = w_in.shape[1] // PLACES
    group_rows = PLACES * local_rows

    def buffer(columns):
        return jnp.zeros((group_rows, columns), jnp.bfloat16)

    def by_part(rows):
        return [rows[a * local_rows : b * local_rows] for a, b in PARTS]

    order = [[SNAKE[(SNAKE.index(i) + s) % PLACES] for s in SHIFTS] for i in range(PLACES)]
    sources = jnp.asarray(order, jnp.int32)[my_tp]
    picked = (sources[:, None] == jnp.arange(PLACES, dtype=jnp.int32)[None, :]).astype(jnp.int32)

    def in_order(blocks):
        blocks = jnp.sum(picked[:, :, None, None] * blocks.reshape(1, PLACES, sp, -1), axis=1)
        mine = lax.dynamic_index_in_dim(blocks, my_sp, 1, keepdims=False).reshape(-1)
        return mine, blocks.transpose(1, 0, 2).reshape(-1)

    query_seg, key_seg = in_order(block_seg[0])
    query_pos, key_pos = in_order(block_pos[0])
    first_head = jnp.full((1,), my_tp * my_heads, jnp.int32)
    table = jnp.concatenate([query_pos, query_seg, key_pos, key_seg, first_head])

    small = [ln1_gain, ln1_bias, b_out, ln2_gain, ln2_bias, b_down, b_qv, b_in]
    sizes = [v.shape[0] for v in small]
    cuts = [sum(sizes[:i]) for i in range(len(sizes) + 1)]
    own, own_cot = tokens[0], cotangent[0]

    low1, high1 = hop(own, own)
    down_slice = lax.all_gather(half(w_down), TOKENS, axis=0, tiled=True)
    small_own, qkv_pieces = fence(half(jnp.concatenate(small)), by_place(w_qkv, 3))
    qkv_pieces = exchange(qkv_pieces)
    gathered = gather_small(small_own[None], bits_of(EVERY))
    low2, high2 = hop(low1, high1)
    in_pieces = by_place(w_in, 1)
    (
        low1,
        high1,
        low2,
        high2,
        qkv_pieces,
        in_pieces,
        gathered,
        down_slice,
        w_out,
        own_cot,
    ) = fence(
        low1,
        high1,
        low2,
        high2,
        qkv_pieces,
        in_pieces,
        gathered,
        down_slice,
        w_out,
        own_cot,
    )
    gathered = full(gathered)
    gain1, bias1, out_bias, gain2, bias2, down_bias, qv_bias, in_bias = (
        gathered[:, cuts[i] : cuts[i + 1]].reshape(-1) for i in range(len(sizes))
    )
    qv_bias = lax.dynamic_slice_in_dim(qv_bias.reshape(2, width), my_tp * head_cols, head_cols, 1)
    in_bias = lax.dynamic_slice_in_dim(in_bias, my_tp * hidden, hidden)

    def norm1(rows):
        return half(normalize(full(rows))[0] * gain1 + bias1)

    in_pieces = exchange(in_pieces)
    qkv_slice = gather_rows(qkv_pieces)
    out_slice = lax.all_gather(half(w_out), TOKENS, axis=0, tiled=True)
    token_parts = [own, join((low1, high1)), join((low2, high2))]
    low3, high3 = hop(low2, high2)
    normed = [norm1(part) for part in token_parts]
    low3, high3, own_cot, *normed = fence(low3, high3, own_cot, *normed)
    low4, high4 = last_hop(low3, high3)
    token_parts.append(join((low3, high3)))
    normed.append(norm1(token_parts[3]))
    blank = jnp.zeros((head_cols,), jnp.float32)
    qkv_bias = jnp.concatenate([qv_bias[0], blank, qv_bias[1]])
    mixed = [half(dot(part, qkv_slice, 1, 0) + qkv_bias) for part in normed]
    low4, high4, own_cot, qkv_slice, *mixed = fence(low4, high4, own_cot, qkv_slice, *mixed)

    cot_low1, cot_high1 = hop(own_cot, own_cot)
    token_parts.append(join((low4, high4)))
    normed.append(norm1(token_parts[4]))
    mixed = jnp.concatenate([*mixed, half(dot(normed[4], qkv_slice, 1, 0) + qkv_bias)])
    mixed, cot_low1, cot_high1, in_pieces, out_slice = fence(
        mixed, cot_low1, cot_high1, in_pieces, out_slice
    )
    in_slice = gather_rows(in_pieces)
    cot_low2, cot_high2 = hop(cot_low1, cot_high1)
    keys = mixed
    if sp > 1:
        keys = lax.all_gather(mixed[:, head_cols:], "sp", axis=0, tiled=True)
    first_key = my_heads if sp == 1 else 0
    attended, level = attention(table, heads, my_heads, mixed, keys, first_key)
    attended, cot_low2, cot_high2 = fence(attended, cot_low2, cot_high2)

    attended_parts = by_part(attended)
    branch_parts = [dot(attended_parts[i], out_slice, 1, 0, jnp.bfloat16) for i in range(5)]
    branch_low, branch_high = hop(*jnp.split(branch_parts[4], 2))
    cot_low3, cot_high3 = hop(cot_low2, cot_high2)
    branch_low, branch_high, cot_low3, cot_high3, *branch_parts = fence(
        branch_low, branch_high, cot_low3, cot_high3, *branch_parts
    )
    up, down = hop(*first_sum(branch_parts[3], branch_low, branch_high))
    cot_low4, cot_high4 = last_hop(cot_low3, cot_high3)
    up, down, cot_low4, cot_high4, in_slice = fence(up, down, cot_low4, cot_high4, in_slice)
    up, down = hop(*next_sum(branch_parts[2], up, down))
    cot_parts = [own_cot, join((cot_low1, cot_high1)), join((cot_low2, cot_high2))]
    cot_parts += [join((cot_low3, cot_high3)), join((cot_low4, cot_high4))]
    up, down, *cot_parts = fence(up, down, *cot_parts)
    up, down = fence(*hop(*next_sum(branch_parts[1], up, down)))
    residual = full(own) + last_sum(branch_parts[0], up, down) + out_bias

    own_normed2, scale2 = normalize(residual)
    second = half(own_normed2 * gain2 + bias2)
    second_parts, act_parts, d_pre_parts, d_second_parts, ffn_parts = [second], [], [], [], []
    low, high = second, second
    for index in range(5):
        if index < 3:
            new_low, new_high = hop(low, high)
        elif index == 3:
            new_low, new_high = last_hop(low, high)
        if index:
            second_parts.append(join((low, high)))
        pre_act = dot(second_parts[index], in_slice, 1, 0) + in_bias
        act, gelu_back = jax.vjp(lambda v: jax.nn.gelu(v, approximate=True), pre_act)
        act_parts.append(half(act))
        d_pre = half(gelu_back(dot(cot_parts[index], down_slice, 1, 1))[0])
        d_pre_parts.append(d_pre)
        d_second_parts.append(dot(d_pre, in_slice, 1, 1, jnp.bfloat16))
        made = [act_parts, d_pre_parts, d_second_parts]
        if index < 3:
            ffn_parts.append(dot(act_parts[index], down_slice, 1, 0, jnp.bfloat16))
            made.append(ffn_parts)
        if index < 4:
            low, high, *held = fence(new_low, new_high, *[parts[index] for parts in made])
            for parts, value in zip(made, held, strict=True):
                parts[index] = value

    low, high = hop(*jnp.split(d_second_parts[4], 2))
    ffn_parts += [dot(act, down_slice, 1, 0, jnp.bfloat16) for act in act_parts[3:]]
    low, high, d_pre_parts[4], act_parts[4], *ffn_parts = fence(
        low, high, d_pre_parts[4], act_parts[4], *ffn_parts
    )
    up, down = hop(*first_sum(d_second_parts[3], low, high))
    out_up, out_down = hop(*jnp.split(ffn_parts[4], 2))
    grad_in = rows_product(second_parts, d_pre_parts, 512, "grad_in")
    grad_in = grad_in.reshape(PLACES, -1, hidden)
    up, down, out_up, out_down, grad_in = fence(up, down, out_up, out_down, grad_in)
    grad_in = lax.psum_scatter(grad_in, TOKENS, scatter_dimension=1, tiled=True)
    up, down = hop(*next_sum(d_second_parts[2], up, down))
    out_up, out_down = hop(*first_sum(ffn_parts[3], out_up, out_down))
    up, down, out_up, out_down, act_parts[4] = fence(up, down, out_up, out_down, act_parts[4])
    up, down = hop(*next_sum(d_second_parts[1], up, down))
    out_up, out_down = hop(*next_sum(ffn_parts[2], out_up, out_down))
    grad_down = rows_product(act_parts, cot_parts, 256, "grad_down")
    grad_b_in = sum(jnp.sum(full(part), axis=0) for part in d_pre_parts)
    blank = jnp.zeros((PLACES * hidden,), jnp.float32)
    grad_b_in = lax.dynamic_update_slice_in_dim(blank, grad_b_in, my_tp * hidden, 0)
    g_b_down = jnp.sum(full(own_cot), axis=0)
    up, down, out_up, out_down, grad_down, grad_b_in = fence(
        up, down, out_up, out_down, grad_down, grad_b_in
    )
    grad_down = lax.psum_scatter(grad_down, TOKENS, scatter_dimension=0, tiled=True)

    d_residual, d_branch, g_b_out, g_gain2, g_bias2 = norm_back(
        (d_second_parts[0], up, down), residual, gain2, own_cot, "norm2_back", True
    )
    low, high = hop(d_branch, d_branch)
    out_up, out_down = next_sum(ffn_parts[1], out_up, out_down)
    low, high, out_up, out_down = fence(low, high, out_up, out_down)
    d_branch_parts, d_attended = [d_branch], [dot(d_branch, out_slice, 1, 1, jnp.bfloat16)]
    for index in range(1, 5):
        d_branch_parts.append(join((low, high)))
        d_attended.append(dot(d_branch_parts[index], out_slice, 1, 1, jnp.bfloat16))
        if index < 3:
            low, high = hop(low, high)
            low, high, grad_in, d_attended[index] = fence(low, high, grad_in, d_attended[index])
        elif index == 3:
            low, high = last_hop(low, high)
            low, high, grad_in, d_attended[index], out_up, out_down = fence(
                low, high, grad_in, d_attended[index], out_up, out_down
            )
            grad_in = exchange(grad_in)

    out_up, out_down = hop(out_up, out_down)
    grads = attention(table, heads, my_heads, mixed, keys, first_key, d_attended, level)
    if sp == 1:
        (d_mixed,) = grads
    else:
        d_keys = half(lax.psum_scatter(full(grads[1]), "sp", scatter_dimension=0, tiled=True))
        d_mixed = jnp.concatenate([grads[0], d_keys], axis=1)
    d_mixed, d_branch_parts[4], grad_down, out_up, out_down = fence(
        d_mixed, d_branch_parts[4], grad_down, out_up, out_down
    )

    mixed_parts = by_part(d_mixed)
    far = dot(mixed_parts[4], qkv_slice, 1, 1, jnp.bfloat16)
    low, high = hop(*jnp.split(far, 2))
    (near,) = products(mixed_parts[3:4], qkv_slice, "d_normed_near")
    grad_qkv = rows_product(normed, mixed_parts, 512, "grad_qkv")
    grad_qkv = grad_qkv.reshape(PLACES, -1, 3 * head_cols)
    low, high, near, grad_qkv, mixed_parts[0] = fence(low, high, near, grad_qkv, mixed_parts[0])
    grad_qkv = lax.psum_scatter(grad_qkv, TOKENS, scatter_dimension=1, tiled=True)
    up, down = hop(*first_sum(near, low, high))
    d_normed = [*products(mixed_parts[:3], qkv_slice, "d_normed"), near, far]
    g_gain1, g_bias1, mixed_sum = norm_sums(d_normed, token_parts, mixed_parts, "norm1_sums")
    up, down, grad_in, g_gain1, g_bias1, mixed_sum, *d_normed[:3] = fence(
        up, down, grad_in, g_gain1, g_bias1, mixed_sum, *d_normed[:3]
    )
    up, down = hop(*next_sum(d_normed[2], up, down))
    grad_out = rows_product(attended_parts, d_branch_parts, 128, "grad_out")
    grad_w_in = from_places(grad_in, 1, "in_back")
    grad_b_qv = jnp.zeros((2, width), jnp.float32)
    for i in range(2):
        piece = mixed_sum[:, 2 * i * head_cols : (2 * i + 1) * head_cols]
        grad_b_qv = lax.dynamic_update_slice(grad_b_qv, piece, (i, my_tp * head_cols))
    whole = [g_gain1, g_bias1, g_b_out, g_gain2, g_bias2, g_b_down, grad_b_qv, grad_b_in]
    summed = rows_by_place([v.reshape(1, -1) for v in whole], "sums_by_place")
    summed = sum_small(summed, TOKENS)
    own_rows = grad_qkv.shape[1]
    grad_qkv = with_rows(grad_qkv, summed, "qkv_with_sums")
    up, down, grad_out, grad_w_in, grad_qkv = fence(up, down, grad_out, grad_w_in, grad_qkv)
    up, down = hop(*next_sum(d_normed[1], up, down))
    grad_qkv = exchange(grad_qkv)
    grad_w_down = converted(grad_down, "down_back")
    output = total((ffn_parts[0], out_up, out_down), residual, down_bias, "output")
    up, down, grad_w_down, output, grad_qkv = fence(up, down, grad_w_down, output, grad_qkv)
    grad_out = lax.psum_scatter(grad_out, TOKENS, scatter_dimension=0, tiled=True)
    grad_tokens = norm_back((d_normed[0], up, down), own, gain1, d_residual, "norm1_back", False)[0]
    grad_w_out = converted(grad_out, "out_back")
    grad_w_qkv, summed = from_places_and_rows(
        grad_qkv, 3, own_rows, summed.shape[1], "qkv_back"
    )
    near_devices = sp * fs
    place = my_sp * fs + lax.axis_index("fs")
    g_gain1, g_bias1, g_b_out, g_gain2, g_bias2, g_b_down, g_b_qv, g_b_in = (
        lax.dynamic_slice_in_dim(summed, cuts[i] * near_devices + place * sizes[i], sizes[i], 1)[0]
        for i in range(len(sizes))
    )
    return (
        output[None],
        grad_tokens[None],
        g_gain1,
        g_bias1,
        grad_w_qkv,
        g_b_qv,
        grad_w_out,
        g_b_out,
        g_gain2,
        g_bias2,
        grad_w_in,
        g_b_in,
        grad_w_down,
        g_b_down,
    )


def solution(mesh):
    ctx, fs = mesh.shape["ctx"], mesh.shape["fsdp"]
    inner = Mesh(mesh.devices.reshape(PLACES, ctx // PLACES, fs), EVERY)
    rows = P("fs", ("tp", "sp"), None)
    vector, matrix, blocks = P(EVERY), P(EVERY, None), P("fs", None)
    kinds = (
        rows,
        vector,
        vector,
        matrix,
        vector,
        matrix,
        vector,
        vector,
        vector,
        matrix,
        vector,
        matrix,
        vector,
    )
    return jax.shard_map(
        on_device,
        mesh=inner,
        in_specs=kinds + (rows, blocks, blocks),
        out_specs=(rows,) + kinds,
        check_vma=False,
    )
```

```python
import functools
import math

import jax
import jax.numpy as jnp
from jax import lax
from jax.experimental import pallas as pl
from jax.experimental.pallas import tpu as pltpu
from jax.sharding import Mesh
from jax.sharding import PartitionSpec as P

HD = 128
BLK = 128
EPSILON = 1e-05
NEG_FILL = -1e30

EVERY = ("tp", "sp", "fs")
TOKENS = ("sp", "fs")
SNAKE = (0, 2, 4, 6, 7, 5, 3, 1)
PLACES = len(SNAKE)
SHIFTS = (0, -1, 1, -2, 2, -3, 3, 4)
PARTS = ((0, 1), (1, 3), (3, 5), (5, 7), (7, 8))


def half(values):
    return values.astype(jnp.bfloat16)


def full(values):
    return values.astype(jnp.float32)


def dot(left, right, left_dim, right_dim, out=jnp.float32):
    return lax.dot_general(
        left, right, (((left_dim,), (right_dim,)), ((), ())), preferred_element_type=jnp.float32
    ).astype(out)


def fence(*values):
    return lax.optimization_barrier(values)


def normalize(values):
    center = values - jnp.mean(values, axis=-1, keepdims=True)
    spread = jnp.mean(center * center, axis=-1, keepdims=True)
    scale = lax.rsqrt(spread + EPSILON)
    return center * scale, scale


def normalize_back(normed, scale, grad):
    return scale * (
        grad
        - jnp.mean(grad, axis=-1, keepdims=True)
        - normed * jnp.mean(grad * normed, axis=-1, keepdims=True)
    )


def hop(upward, downward):
    up = [(SNAKE[i], SNAKE[(i + 1) % PLACES]) for i in range(PLACES)]
    down = [(b, a) for a, b in up]
    return lax.ppermute(upward, "tp", up), lax.ppermute(downward, "tp", down)


def last_hop(below, above):
    n = below.shape[0] // 2
    return hop(below[:n], above[n:])


def first_sum(part, low, high):
    below, above = jnp.split(part, 2)
    n = below.shape[0] // 2
    upward = jnp.concatenate([half(full(above[:n]) + full(low)), above[n:]])
    downward = jnp.concatenate([below[:n], half(full(below[n:]) + full(high))])
    return upward, downward


def next_sum(part, upward, downward):
    below, above = jnp.split(part, 2)
    return half(full(above) + full(upward)), half(full(below) + full(downward))


def last_sum(part, upward, downward):
    return full(part) + full(upward) + full(downward)


def join(pair):
    return jnp.concatenate(pair)


def put(buffer, part, index, local_rows):
    return lax.dynamic_update_slice_in_dim(buffer, part, PARTS[index][0] * local_rows, 0)


def bits_of(names):
    return [
        (name, 1 << bit, lax.axis_size(name))
        for name in reversed(names)
        for bit in range(lax.axis_size(name).bit_length() - 1)
    ]


def swap(values, name, bit, size):
    return lax.ppermute(values, name, [(i, i ^ bit) for i in range(size)])


def gather_small(values, bits):
    for name, bit, size in bits:
        other = swap(values, name, bit, size)
        first = (lax.axis_index(name) & bit) == 0
        values = jnp.concatenate([jnp.where(first, values, other), jnp.where(first, other, values)])
    return values


def sum_small(values, names):
    for name, bit, size in bits_of(names):
        values = values + swap(values, name, bit, size)
    return values


def by_place(rows, groups):
    n, width = rows.shape
    part = width // groups // PLACES
    rows = half(rows).reshape(n, groups, PLACES, part).transpose(2, 0, 1, 3)
    return rows.reshape(PLACES, n, groups * part)


def exchange(pieces):
    return lax.all_to_all(pieces, "tp", split_axis=0, concat_axis=0, tiled=True)


def in_hbm(*arrays):
    return [pltpu.with_memory_space_constraint(v, pltpu.HBM) for v in arrays]


def settings(name, megabytes=40):
    return {
        "compiler_params": pltpu.CompilerParams(vmem_limit_bytes=megabytes << 20),
        "cost_estimate": pl.CostEstimate(flops=1 << 20, bytes_accessed=1 << 20, transcendentals=0),
        "name": name,
    }


def rows_product(lefts, rights, tile, name):
    count, out_rows, out_cols = len(lefts), lefts[0].shape[1], rights[0].shape[1]

    def body(*refs):
        total = None
        for left, right in zip(refs[:count], refs[count : 2 * count], strict=True):
            term = lax.dot_general(
                left[...],
                right[...],
                (((0,), (0,)), ((), ())),
                preferred_element_type=jnp.float32,
            )
            total = term if total is None else total + term
        refs[2 * count][...] = half(total)

    return pl.pallas_call(
        body,
        grid=(out_rows // tile,),
        in_specs=[pl.BlockSpec((v.shape[0], tile), lambda i: (0, i)) for v in lefts]
        + [pl.BlockSpec(v.shape, lambda i: (0, 0)) for v in rights],
        out_specs=pl.BlockSpec((tile, out_cols), lambda i: (i, 0)),
        out_shape=pltpu.HBM((out_rows, out_cols), jnp.bfloat16),
        **settings(name),
    )(*lefts, *rights)


def score_rows(table, keys, queries, heads, query_blocks):
    scores = dot(keys, queries, 1, 1)
    count, key_blocks = queries.shape[0] // BLK, keys.shape[0] // BLK
    lane = lax.broadcasted_iota(jnp.int32, (1, queries.shape[0]), 1)
    down = lax.broadcasted_iota(jnp.int32, (BLK, queries.shape[0]), 0)
    ahead = down - lax.rem(lane, BLK)
    head = table[2 * query_blocks + 2 * key_blocks] + pl.program_id(0)
    slope = jnp.exp2(full(jnp.full(down.shape, head + 1, jnp.int32)) * (-8.0 / heads))
    slant = slope * full(down)
    tiles = []
    for j in range(key_blocks):
        key_pos = table[2 * query_blocks + j]
        key_seg = table[2 * query_blocks + key_blocks + j]
        limit = jnp.zeros((1, queries.shape[0]), jnp.int32)
        for i in range(count):
            block = pl.program_id(1) * count + i
            seen = (key_seg == 0) | (key_seg == table[query_blocks + block])
            here = jnp.where(seen, table[block] - key_pos, -BLK)
            limit = jnp.where(lane >= i * BLK, here, limit)
        tile = scores[j * BLK : (j + 1) * BLK] * (1.0 / math.sqrt(HD))
        tile = tile + (slant + slope * full(key_pos))
        tiles.append(jnp.where(ahead <= limit, tile, NEG_FILL))
    return jnp.concatenate(tiles)


def attend_body(heads, query_blocks, table, query, key, value, attended, level, value_t):
    @pl.when(pl.program_id(1) == 0)
    def turn():
        value_t[...] = half(full(value[...]).T)

    scores = score_rows(table, key[...], query[...], heads, query_blocks)
    top = jnp.max(scores, axis=0, keepdims=True)
    expon = jnp.exp(scores - top)
    total = jnp.sum(expon, axis=0, keepdims=True)
    probs = half(expon * (1.0 / total))
    attended[...] = half(dot(value_t[...], probs, 1, 0).T)
    level[...] = (top + jnp.log(total))[None]


def attend_back_body(
    heads,
    query_blocks,
    my_heads,
    split,
    table,
    query,
    key,
    value,
    level,
    *rest,
):
    rest, grad_parts = rest[len(PARTS) :], rest[: len(PARTS)]
    d_query, d_keys = (rest[0], rest[1]) if split else (rest[0], rest[0])
    grads, key_t, key_acc, value_acc = rest[-4:]
    head, block = pl.program_id(0), pl.program_id(1)
    rows = query.shape[0]
    scale = 1.0 / math.sqrt(HD)

    def columns(place):
        return pl.ds(pl.multiple_of((place * my_heads + head) * HD, HD), HD)

    @pl.when(block == 0)
    def begin():
        begin_row = 0
        for part in grad_parts:
            grads[begin_row : begin_row + part.shape[0], :] = part[...]
            begin_row += part.shape[0]
        key_t[...] = half(full(key[...]).T)
        key_acc[...] = jnp.zeros_like(key_acc)
        value_acc[...] = jnp.zeros_like(value_acc)

    scores = score_rows(table, key[...], query[...], heads, query_blocks)
    probs = jnp.exp(scores - level[0])
    grad = grads[pl.ds(pl.multiple_of(block * rows, rows), rows), :]
    d_probs = dot(value[...], grad, 1, 1)
    delta = jnp.sum(probs * d_probs, axis=0, keepdims=True)
    d_scores = half(probs * (d_probs - delta))
    turned = (dot(key_t[...], d_scores, 1, 0) * scale).T
    d_query[pl.ds(pl.multiple_of(block * rows, rows), rows), columns(0)] = half(turned)
    key_acc[...] += dot(d_scores, query[...], 1, 0)
    value_acc[...] += dot(half(probs), grad, 1, 0)

    @pl.when(block == pl.num_programs(1) - 1)
    def end():
        shift = 0 if split else 1
        d_keys[:, columns(shift)] = half(key_acc[...] * scale)
        d_keys[:, columns(shift + 1)] = half(value_acc[...])


def attention(table, heads, my_heads, query, keys, first, grad=None, level=None):
    rows, total = query.shape[0], keys.shape[0]
    step = 256 if total <= 1024 else BLK
    columns = my_heads * HD
    scalars = pl.BlockSpec(memory_space=pltpu.SMEM)
    of_query = pl.BlockSpec((step, HD), lambda h, i: (i, h))
    of_level = pl.BlockSpec((1, 1, step), lambda h, i: (h, 0, i))
    in_specs = [
        scalars,
        of_query,
        pl.BlockSpec((total, HD), lambda h, i: (0, first + h)),
        pl.BlockSpec((total, HD), lambda h, i: (0, first + my_heads + h)),
    ]
    common = {
        "grid": (my_heads, rows // step),
        "compiler_params": pltpu.CompilerParams(vmem_limit_bytes=48 << 20),
        "cost_estimate": pl.CostEstimate(
            flops=(4 if grad is None else 10) * rows * total * columns,
            bytes_accessed=32 << 20,
            transcendentals=my_heads * rows * total,
        ),
    }
    if grad is None:
        return pl.pallas_call(
            functools.partial(attend_body, heads, rows // BLK),
            in_specs=in_specs,
            out_specs=[of_query, of_level],
            out_shape=[
                jax.ShapeDtypeStruct((rows, columns), jnp.bfloat16),
                jax.ShapeDtypeStruct((my_heads, 1, rows), jnp.float32),
            ],
            scratch_shapes=[pltpu.VMEM((HD, total), jnp.bfloat16)],
            name="attend",
            **common,
        )(table, *in_hbm(query, keys, keys))
    split = query is not keys
    shapes = [(rows, columns), (total, 2 * columns)] if split else [(rows, 3 * columns)]
    return pl.pallas_call(
        functools.partial(attend_back_body, heads, rows // BLK, my_heads, split),
        in_specs=in_specs
        + [of_level]
        + [pl.BlockSpec((part.shape[0], HD), lambda h, i: (0, h)) for part in grad],
        out_specs=[pl.BlockSpec(shape, lambda h, i: (0, 0)) for shape in shapes],
        out_shape=[jax.ShapeDtypeStruct(shape, jnp.bfloat16) for shape in shapes],
        scratch_shapes=[
            pltpu.VMEM((rows, HD), jnp.bfloat16),
            pltpu.VMEM((HD, total), jnp.bfloat16),
            pltpu.VMEM((total, HD), jnp.float32),
            pltpu.VMEM((total, HD), jnp.float32),
        ],
        name="attend_back",
        **common,
    )(table, *in_hbm(query, keys, keys, level, *grad))


def products(parts, matrix, name):
    count, tile = len(parts), 512

    def body(*refs):
        for part, out in zip(refs[:count], refs[count + 1 :], strict=True):
            out[...] = dot(part[...], refs[count][...], 1, 1, jnp.bfloat16)

    return pl.pallas_call(
        body,
        grid=(matrix.shape[0] // tile,),
        in_specs=[pl.BlockSpec(v.shape, lambda i: (0, 0)) for v in parts]
        + [pl.BlockSpec((tile, matrix.shape[1]), lambda i: (i, 0))],
        out_specs=[pl.BlockSpec((v.shape[0], tile), lambda i: (0, i)) for v in parts],
        out_shape=[
            jax.ShapeDtypeStruct((v.shape[0], matrix.shape[0]), jnp.bfloat16) for v in parts
        ],
        **settings(name),
    )(*parts, matrix)


def gather_rows(rows):
    rows = lax.all_gather(rows, TOKENS, axis=1, tiled=True)
    return rows.reshape(-1, rows.shape[2])


def from_places(grad, groups, name):
    places, n, width = grad.shape
    part = width // groups

    def body(grad_ref, out_ref):
        for group in range(groups):
            for place in range(places):
                begin = (group * places + place) * part
                out_ref[:, begin : begin + part] = full(
                    grad_ref[place, :, group * part : (group + 1) * part]
                )

    return pl.pallas_call(
        body,
        out_shape=jax.ShapeDtypeStruct((n, places * width), jnp.float32),
        **settings(name),
    )(grad)


def norm_back(sums, rows, gain, direct, name, branch):
    n, width = rows.shape
    step = 64

    def body(part, upward, downward, rows_ref, gain_ref, direct_ref, grad_ref, *rest):
        @pl.when(pl.program_id(0) == 0)
        def begin():
            for ref in rest[-3 if branch else -2 :]:
                ref[...] = jnp.zeros_like(ref)

        grad = full(part[...]) + full(upward[...]) + full(downward[...])
        normed, scale = normalize(full(rows_ref[...]))
        out = full(direct_ref[...]) + normalize_back(normed, scale, grad * gain_ref[...])
        grad_ref[...] = out
        if branch:
            rounded = half(out)
            rest[0][...] = rounded
            rest[-3][...] += jnp.sum(full(rounded), axis=0, keepdims=True)
        rest[-2][...] += jnp.sum(grad * normed, axis=0, keepdims=True)
        rest[-1][...] += jnp.sum(grad, axis=0, keepdims=True)

    tile = pl.BlockSpec((step, width), lambda i: (i, 0))
    line = pl.BlockSpec((1, width), lambda i: (0, 0))
    lines = 3 if branch else 2
    return pl.pallas_call(
        body,
        grid=(n // step,),
        in_specs=[tile] * 4 + [line, tile],
        out_specs=[tile] * (2 if branch else 1) + [line] * lines,
        out_shape=[jax.ShapeDtypeStruct((n, width), jnp.float32)]
        + [jax.ShapeDtypeStruct((n, width), jnp.bfloat16)] * branch
        + [jax.ShapeDtypeStruct((1, width), jnp.float32)] * lines,
        **settings(name),
    )(*sums, rows, gain.reshape(1, -1), direct)


def converted(values, name):
    def body(values_ref, out_ref):
        out_ref[...] = full(values_ref[...])

    return pl.pallas_call(
        body, out_shape=jax.ShapeDtypeStruct(values.shape, jnp.float32), **settings(name)
    )(values)


def total(sums, rows, bias, name):
    def body(part, upward, downward, rows_ref, bias_ref, out_ref):
        out = full(part[...]) + full(upward[...]) + full(downward[...])
        out_ref[...] = half(rows_ref[...] + out + bias_ref[...])

    return pl.pallas_call(
        body, out_shape=jax.ShapeDtypeStruct(rows.shape, jnp.bfloat16), **settings(name)
    )(*sums, rows, bias.reshape(1, -1))


def rows_by_place(vectors, name):
    widths = [v.shape[1] // PLACES for v in vectors]

    def body(*refs):
        begin = 0
        for ref, width in zip(refs[:-1], widths, strict=True):
            for place in range(PLACES):
                refs[-1][place : place + 1, begin : begin + width] = ref[
                    :, place * width : (place + 1) * width
                ]
            begin += width

    return pl.pallas_call(
        body,
        out_shape=jax.ShapeDtypeStruct((PLACES, sum(widths)), jnp.float32),
        **settings(name),
    )(*vectors)


def with_rows(pieces, rows, name):
    places, n, width = pieces.shape
    more = -(-rows.shape[1] // width)
    padded = -(-more // 8) * 8

    def body(pieces_ref, rows_ref, out_ref):
        out_ref[:, :n, :] = pieces_ref[...]
        out_ref[:, n:, :] = jnp.zeros((places, padded, width), jnp.bfloat16)
        for place in range(places):
            lines = [
                rows_ref[place : place + 1, i * width : (i + 1) * width] for i in range(more)
            ]
            lines.append(jnp.zeros((padded - more, width), jnp.float32))
            out_ref[place, n:, :] = half(jnp.concatenate(lines))

    return pl.pallas_call(
        body,
        out_shape=jax.ShapeDtypeStruct((places, n + padded, width), jnp.bfloat16),
        **settings(name),
    )(pieces, rows)


def from_places_and_rows(received, groups, n, count, name):
    places, padded, width = received.shape
    part = width // groups
    more = count // width

    def body(received_ref, out_ref, sum_ref):
        for group in range(groups):
            for place in range(places):
                begin = (group * places + place) * part
                out_ref[:, begin : begin + part] = full(
                    received_ref[place, :n, group * part : (group + 1) * part]
                )
        lines = jnp.sum(full(received_ref[:, n:, :]), axis=0)
        for i in range(more):
            sum_ref[:, i * width : (i + 1) * width] = lines[i : i + 1]

    return pl.pallas_call(
        body,
        out_shape=[
            jax.ShapeDtypeStruct((n, places * width), jnp.float32),
            jax.ShapeDtypeStruct((1, count), jnp.float32),
        ],
        **settings(name),
    )(received)


def norm_sums(grads, rows, mixed, name):
    width, count, step = rows[0].shape[1], len(rows), 64
    columns = mixed[0].shape[1]

    def body(*refs):
        gain = jnp.zeros((1, width), jnp.float32)
        bias = jnp.zeros((1, width), jnp.float32)
        for grad_ref, rows_ref in zip(refs[:count], refs[count : 2 * count], strict=True):

            def add(i, carried, grad_ref=grad_ref, rows_ref=rows_ref):
                here = pl.ds(pl.multiple_of(i * step, step), step)
                grad = full(grad_ref[here, :])
                normed = normalize(full(rows_ref[here, :]))[0]
                return (
                    carried[0] + jnp.sum(grad * normed, axis=0, keepdims=True),
                    carried[1] + jnp.sum(grad, axis=0, keepdims=True),
                )

            gain, bias = lax.fori_loop(0, rows_ref.shape[0] // step, add, (gain, bias))
        refs[-3][...] = gain
        refs[-2][...] = bias
        refs[-1][...] = sum(
            jnp.sum(full(ref[...]), axis=0, keepdims=True) for ref in refs[2 * count : 3 * count]
        )

    return pl.pallas_call(
        body,
        out_shape=[jax.ShapeDtypeStruct((1, width), jnp.float32)] * 2
        + [jax.ShapeDtypeStruct((1, columns), jnp.float32)],
        **settings(name),
    )(*grads, *rows, *mixed)


def on_device(
    tokens,
    ln1_gain,
    ln1_bias,
    w_qkv,
    b_qv,
    w_out,
    b_out,
    ln2_gain,
    ln2_bias,
    w_in,
    b_in,
    w_down,
    b_down,
    cotangent,
    block_seg,
    block_pos,
):
    sp = lax.axis_size("sp")
    fs = lax.axis_size("fs")
    devices = PLACES * sp * fs
    my_tp = lax.axis_index("tp")
    my_sp = lax.axis_index("sp")
    local_rows, width = tokens.shape[1:]
    heads = width // HD
    my_heads = heads // PLACES
    head_cols = my_heads * HD
    hidden = w_in.shape[1] // PLACES
    group_rows = PLACES * local_rows

    def buffer(columns):
        return jnp.zeros((group_rows, columns), jnp.bfloat16)

    def by_part(rows):
        return [rows[a * local_rows : b * local_rows] for a, b in PARTS]

    order = [[SNAKE[(SNAKE.index(i) + s) % PLACES] for s in SHIFTS] for i in range(PLACES)]
    sources = jnp.asarray(order, jnp.int32)[my_tp]
    picked = (sources[:, None] == jnp.arange(PLACES, dtype=jnp.int32)[None, :]).astype(jnp.int32)

    def in_order(blocks):
        blocks = jnp.sum(picked[:, :, None, None] * blocks.reshape(1, PLACES, sp, -1), axis=1)
        mine = lax.dynamic_index_in_dim(blocks, my_sp, 1, keepdims=False).reshape(-1)
        return mine, blocks.transpose(1, 0, 2).reshape(-1)

    query_seg, key_seg = in_order(block_seg[0])
    query_pos, key_pos = in_order(block_pos[0])
    first_head = jnp.full((1,), my_tp * my_heads, jnp.int32)
    table = jnp.concatenate([query_pos, query_seg, key_pos, key_seg, first_head])

    small = [ln1_gain, ln1_bias, b_out, ln2_gain, ln2_bias, b_down, b_qv, b_in]
    sizes = [v.shape[0] for v in small]
    cuts = [sum(sizes[:i]) for i in range(len(sizes) + 1)]
    own, own_cot = tokens[0], cotangent[0]

    low1, high1 = hop(own, own)
    down_slice = lax.all_gather(half(w_down), TOKENS, axis=0, tiled=True)
    small_own, qkv_pieces = fence(half(jnp.concatenate(small)), by_place(w_qkv, 3))
    qkv_pieces = exchange(qkv_pieces)
    gathered = gather_small(small_own[None], bits_of(EVERY))
    low2, high2 = hop(low1, high1)
    in_pieces = by_place(w_in, 1)
    (
        low1,
        high1,
        low2,
        high2,
        qkv_pieces,
        in_pieces,
        gathered,
        down_slice,
        w_out,
        own_cot,
    ) = fence(
        low1,
        high1,
        low2,
        high2,
        qkv_pieces,
        in_pieces,
        gathered,
        down_slice,
        w_out,
        own_cot,
    )
    gathered = full(gathered)
    gain1, bias1, out_bias, gain2, bias2, down_bias, qv_bias, in_bias = (
        gathered[:, cuts[i] : cuts[i + 1]].reshape(-1) for i in range(len(sizes))
    )
    qv_bias = lax.dynamic_slice_in_dim(qv_bias.reshape(2, width), my_tp * head_cols, head_cols, 1)
    in_bias = lax.dynamic_slice_in_dim(in_bias, my_tp * hidden, hidden)

    def norm1(rows):
        return half(normalize(full(rows))[0] * gain1 + bias1)

    in_pieces = exchange(in_pieces)
    qkv_slice = gather_rows(qkv_pieces)
    out_slice = lax.all_gather(half(w_out), TOKENS, axis=0, tiled=True)
    token_parts = [own, join((low1, high1)), join((low2, high2))]
    low3, high3 = hop(low2, high2)
    normed = [norm1(part) for part in token_parts]
    low3, high3, own_cot, *normed = fence(low3, high3, own_cot, *normed)
    low4, high4 = last_hop(low3, high3)
    token_parts.append(join((low3, high3)))
    normed.append(norm1(token_parts[3]))
    blank = jnp.zeros((head_cols,), jnp.float32)
    qkv_bias = jnp.concatenate([qv_bias[0], blank, qv_bias[1]])
    mixed = [half(dot(part, qkv_slice, 1, 0) + qkv_bias) for part in normed]
    low4, high4, own_cot, qkv_slice, *mixed = fence(low4, high4, own_cot, qkv_slice, *mixed)

    cot_low1, cot_high1 = hop(own_cot, own_cot)
    token_parts.append(join((low4, high4)))
    normed.append(norm1(token_parts[4]))
    mixed = jnp.concatenate([*mixed, half(dot(normed[4], qkv_slice, 1, 0) + qkv_bias)])
    mixed, cot_low1, cot_high1, in_pieces, out_slice = fence(
        mixed, cot_low1, cot_high1, in_pieces, out_slice
    )
    in_slice = lax.all_gather(in_pieces, TOKENS, axis=0, tiled=False)
    in_slice = in_slice.transpose(1, 0, 2, 3).reshape(-1, hidden)
    cot_low2, cot_high2 = hop(cot_low1, cot_high1)
    keys = mixed
    if sp > 1:
        keys = lax.all_gather(mixed[:, head_cols:], "sp", axis=0, tiled=True)
    first_key = my_heads if sp == 1 else 0
    attended, level = attention(table, heads, my_heads, mixed, keys, first_key)
    attended, cot_low2, cot_high2 = fence(attended, cot_low2, cot_high2)

    attended_parts = by_part(attended)
    branch_parts = [dot(attended_parts[i], out_slice, 1, 0, jnp.bfloat16) for i in range(5)]
    branch_low, branch_high = hop(*jnp.split(branch_parts[4], 2))
    cot_low3, cot_high3 = hop(cot_low2, cot_high2)
    branch_low, branch_high, cot_low3, cot_high3, *branch_parts = fence(
        branch_low, branch_high, cot_low3, cot_high3, *branch_parts
    )
    up, down = hop(*first_sum(branch_parts[3], branch_low, branch_high))
    up, down, in_slice = fence(up, down, in_slice)
    up, down = hop(*next_sum(branch_parts[2], up, down))
    cot_parts = [own_cot, join((cot_low1, cot_high1)), join((cot_low2, cot_high2))]
    cot_parts.append(join((cot_low3, cot_high3)))
    up, down, *cot_parts = fence(up, down, *cot_parts)
    up, down = hop(*next_sum(branch_parts[1], up, down))
    up, down, cot_low3, cot_high3 = fence(up, down, cot_low3, cot_high3)
    residual = full(own) + last_sum(branch_parts[0], up, down) + out_bias

    own_normed2, scale2 = normalize(residual)
    second = half(own_normed2 * gain2 + bias2)
    second_parts, act_parts, d_pre_parts, d_second_parts, ffn_parts = [second], [], [], [], []
    low, high = second, second
    for index in range(5):
        if index < 3:
            new_low, new_high = hop(low, high)
        elif index == 3:
            new_low, new_high = last_hop(low, high)
            cot_low4, cot_high4 = last_hop(cot_low3, cot_high3)
        if index:
            second_parts.append(join((low, high)))
        pre_act = dot(second_parts[index], in_slice, 1, 0) + in_bias
        act, gelu_back = jax.vjp(lambda v: jax.nn.gelu(v, approximate=True), pre_act)
        act_parts.append(half(act))
        d_pre = half(gelu_back(dot(cot_parts[index], down_slice, 1, 1))[0])
        d_pre_parts.append(d_pre)
        d_second_parts.append(dot(d_pre, in_slice, 1, 1, jnp.bfloat16))
        made = [act_parts, d_pre_parts, d_second_parts]
        if index < 3:
            ffn_parts.append(dot(act_parts[index], down_slice, 1, 0, jnp.bfloat16))
            made.append(ffn_parts)
        if index < 4:
            low, high, *held = fence(new_low, new_high, *[parts[index] for parts in made])
            for parts, value in zip(made, held, strict=True):
                parts[index] = value
        if index == 3:
            low, cot_low4, cot_high4 = fence(low, cot_low4, cot_high4)
            cot_parts.append(join((cot_low4, cot_high4)))

    low, high = hop(*jnp.split(d_second_parts[4], 2))
    ffn_parts += [dot(act, down_slice, 1, 0, jnp.bfloat16) for act in act_parts[3:]]
    low, high, d_pre_parts[4], act_parts[4], *ffn_parts = fence(
        low, high, d_pre_parts[4], act_parts[4], *ffn_parts
    )
    up, down = hop(*first_sum(d_second_parts[3], low, high))
    out_up, out_down = hop(*jnp.split(ffn_parts[4], 2))
    grad_in = rows_product(second_parts, d_pre_parts, 512, "grad_in")
    grad_in = grad_in.reshape(PLACES, -1, hidden)
    up, down, out_up, out_down, grad_in = fence(up, down, out_up, out_down, grad_in)
    grad_in = lax.psum_scatter(grad_in, TOKENS, scatter_dimension=1, tiled=True)
    up, down = hop(*next_sum(d_second_parts[2], up, down))
    out_up, out_down = hop(*first_sum(ffn_parts[3], out_up, out_down))
    up, down, out_up, out_down, act_parts[4] = fence(up, down, out_up, out_down, act_parts[4])
    up, down = hop(*next_sum(d_second_parts[1], up, down))
    out_up, out_down = hop(*next_sum(ffn_parts[2], out_up, out_down))
    grad_down = rows_product(act_parts, cot_parts, 256, "grad_down")
    grad_b_in = sum(jnp.sum(full(part), axis=0) for part in d_pre_parts)
    blank = jnp.zeros((PLACES * hidden,), jnp.float32)
    grad_b_in = lax.dynamic_update_slice_in_dim(blank, grad_b_in, my_tp * hidden, 0)
    g_b_down = jnp.sum(full(own_cot), axis=0)
    up, down, out_up, out_down, grad_down, grad_b_in = fence(
        up, down, out_up, out_down, grad_down, grad_b_in
    )
    grad_down = lax.psum_scatter(grad_down, TOKENS, scatter_dimension=0, tiled=True)

    d_residual, d_branch, g_b_out, g_gain2, g_bias2 = norm_back(
        (d_second_parts[0], up, down), residual, gain2, own_cot, "norm2_back", True
    )
    low, high = hop(d_branch, d_branch)
    out_up, out_down = next_sum(ffn_parts[1], out_up, out_down)
    low, high, out_up, out_down = fence(low, high, out_up, out_down)
    d_branch_parts, d_attended = [d_branch], [dot(d_branch, out_slice, 1, 1, jnp.bfloat16)]
    for index in range(1, 5):
        d_branch_parts.append(join((low, high)))
        d_attended.append(dot(d_branch_parts[index], out_slice, 1, 1, jnp.bfloat16))
        if index < 3:
            low, high = hop(low, high)
            low, high, grad_in, d_attended[index] = fence(low, high, grad_in, d_attended[index])
        elif index == 3:
            low, high = last_hop(low, high)
            low, high, grad_in, d_attended[index], out_up, out_down = fence(
                low, high, grad_in, d_attended[index], out_up, out_down
            )
            grad_in = exchange(grad_in)

    out_up, out_down = hop(out_up, out_down)
    grads = attention(table, heads, my_heads, mixed, keys, first_key, d_attended, level)
    if sp == 1:
        (d_mixed,) = grads
    else:
        d_keys = half(lax.psum_scatter(full(grads[1]), "sp", scatter_dimension=0, tiled=True))
        d_mixed = jnp.concatenate([grads[0], d_keys], axis=1)
    d_mixed, d_branch_parts[4], grad_down, out_up, out_down = fence(
        d_mixed, d_branch_parts[4], grad_down, out_up, out_down
    )

    mixed_parts = by_part(d_mixed)
    far = dot(mixed_parts[4], qkv_slice, 1, 1, jnp.bfloat16)
    low, high = hop(*jnp.split(far, 2))
    (near,) = products(mixed_parts[3:4], qkv_slice, "d_normed_near")
    grad_qkv = rows_product(normed, mixed_parts, 512, "grad_qkv")
    grad_qkv = grad_qkv.reshape(PLACES, -1, 3 * head_cols)
    low, high, near, grad_qkv, mixed_parts[0] = fence(low, high, near, grad_qkv, mixed_parts[0])
    grad_qkv = lax.psum_scatter(grad_qkv, TOKENS, scatter_dimension=1, tiled=True)
    up, down = hop(*first_sum(near, low, high))
    d_normed = [*products(mixed_parts[:3], qkv_slice, "d_normed"), near, far]
    g_gain1, g_bias1, mixed_sum = norm_sums(d_normed, token_parts, mixed_parts, "norm1_sums")
    grad_out = rows_product(attended_parts, d_branch_parts, 128, "grad_out")
    up, down, grad_in, grad_out, g_gain1, g_bias1, mixed_sum, *d_normed[:3] = fence(
        up, down, grad_in, grad_out, g_gain1, g_bias1, mixed_sum, *d_normed[:3]
    )
    up, down = hop(*next_sum(d_normed[2], up, down))
    grad_b_qv = jnp.zeros((2, width), jnp.float32)
    for i in range(2):
        piece = mixed_sum[:, 2 * i * head_cols : (2 * i + 1) * head_cols]
        grad_b_qv = lax.dynamic_update_slice(grad_b_qv, piece, (i, my_tp * head_cols))
    whole = [g_gain1, g_bias1, g_b_out, g_gain2, g_bias2, g_b_down, grad_b_qv, grad_b_in]
    summed = rows_by_place([v.reshape(1, -1) for v in whole], "sums_by_place")
    summed = sum_small(summed, TOKENS)
    own_rows = grad_qkv.shape[1]
    grad_qkv = with_rows(grad_qkv, summed, "qkv_with_sums")
    up, down, grad_out, grad_in, grad_qkv = fence(up, down, grad_out, grad_in, grad_qkv)
    up, down = hop(*next_sum(d_normed[1], up, down))
    grad_qkv = exchange(grad_qkv)
    grad_w_in = from_places(grad_in, 1, "in_back")
    grad_w_down = converted(grad_down, "down_back")
    output = total((ffn_parts[0], out_up, out_down), residual, down_bias, "output")
    up, down, grad_w_down, grad_w_in, output, grad_qkv = fence(
        up, down, grad_w_down, grad_w_in, output, grad_qkv
    )
    grad_out = lax.psum_scatter(grad_out, TOKENS, scatter_dimension=0, tiled=True)
    grad_tokens = norm_back((d_normed[0], up, down), own, gain1, d_residual, "norm1_back", False)[0]
    grad_w_out = converted(grad_out, "out_back")
    grad_w_qkv, summed = from_places_and_rows(
        grad_qkv, 3, own_rows, summed.shape[1], "qkv_back"
    )
    near_devices = sp * fs
    place = my_sp * fs + lax.axis_index("fs")
    g_gain1, g_bias1, g_b_out, g_gain2, g_bias2, g_b_down, g_b_qv, g_b_in = (
        lax.dynamic_slice_in_dim(summed, cuts[i] * near_devices + place * sizes[i], sizes[i], 1)[0]
        for i in range(len(sizes))
    )
    return (
        output[None],
        grad_tokens[None],
        g_gain1,
        g_bias1,
        grad_w_qkv,
        g_b_qv,
        grad_w_out,
        g_b_out,
        g_gain2,
        g_bias2,
        grad_w_in,
        g_b_in,
        grad_w_down,
        g_b_down,
    )


def solution(mesh):
    ctx, fs = mesh.shape["ctx"], mesh.shape["fsdp"]
    inner = Mesh(mesh.devices.reshape(PLACES, ctx // PLACES, fs), EVERY)
    rows = P("fs", ("tp", "sp"), None)
    vector, matrix, blocks = P(EVERY), P(EVERY, None), P("fs", None)
    kinds = (
        rows,
        vector,
        vector,
        matrix,
        vector,
        matrix,
        vector,
        vector,
        vector,
        matrix,
        vector,
        matrix,
        vector,
    )
    return jax.shard_map(
        on_device,
        mesh=inner,
        in_specs=kinds + (rows, blocks, blocks),
        out_specs=(rows,) + kinds,
        check_vma=False,
    )
```

```python
import functools
import math

import jax
import jax.numpy as jnp
from jax import lax
from jax.experimental import pallas as pl
from jax.experimental.pallas import tpu as pltpu
from jax.sharding import Mesh
from jax.sharding import PartitionSpec as P

HD = 128
BLK = 128
EPSILON = 1e-05
NEG_FILL = -1e30

EVERY = ("tp", "sp", "fs")
TOKENS = ("sp", "fs")
SNAKE = (0, 2, 4, 6, 7, 5, 3, 1)
PLACES = len(SNAKE)
SHIFTS = (0, -1, 1, -2, 2, -3, 3, 4)
PARTS = ((0, 1), (1, 3), (3, 5), (5, 7), (7, 8))


def half(values):
    return values.astype(jnp.bfloat16)


def full(values):
    return values.astype(jnp.float32)


def dot(left, right, left_dim, right_dim, out=jnp.float32):
    return lax.dot_general(
        left, right, (((left_dim,), (right_dim,)), ((), ())), preferred_element_type=jnp.float32
    ).astype(out)


def fence(*values):
    return lax.optimization_barrier(values)


def normalize(values):
    center = values - jnp.mean(values, axis=-1, keepdims=True)
    spread = jnp.mean(center * center, axis=-1, keepdims=True)
    scale = lax.rsqrt(spread + EPSILON)
    return center * scale, scale


def normalize_back(normed, scale, grad):
    return scale * (
        grad
        - jnp.mean(grad, axis=-1, keepdims=True)
        - normed * jnp.mean(grad * normed, axis=-1, keepdims=True)
    )


def hop(upward, downward):
    up = [(SNAKE[i], SNAKE[(i + 1) % PLACES]) for i in range(PLACES)]
    down = [(b, a) for a, b in up]
    return lax.ppermute(upward, "tp", up), lax.ppermute(downward, "tp", down)


def last_hop(below, above):
    n = below.shape[0] // 2
    return hop(below[:n], above[n:])


def first_sum(part, low, high):
    below, above = jnp.split(part, 2)
    n = below.shape[0] // 2
    upward = jnp.concatenate([half(full(above[:n]) + full(low)), above[n:]])
    downward = jnp.concatenate([below[:n], half(full(below[n:]) + full(high))])
    return upward, downward


def next_sum(part, upward, downward):
    below, above = jnp.split(part, 2)
    return half(full(above) + full(upward)), half(full(below) + full(downward))


def last_sum(part, upward, downward):
    return full(part) + full(upward) + full(downward)


def join(pair):
    return jnp.concatenate(pair)


def put(buffer, part, index, local_rows):
    return lax.dynamic_update_slice_in_dim(buffer, part, PARTS[index][0] * local_rows, 0)


def bits_of(names):
    return [
        (name, 1 << bit, lax.axis_size(name))
        for name in reversed(names)
        for bit in range(lax.axis_size(name).bit_length() - 1)
    ]


def swap(values, name, bit, size):
    return lax.ppermute(values, name, [(i, i ^ bit) for i in range(size)])


def gather_small(values, bits):
    for name, bit, size in bits:
        other = swap(values, name, bit, size)
        first = (lax.axis_index(name) & bit) == 0
        values = jnp.concatenate([jnp.where(first, values, other), jnp.where(first, other, values)])
    return values


def sum_small(values, names):
    for name, bit, size in bits_of(names):
        values = values + swap(values, name, bit, size)
    return values


def by_place(rows, groups):
    n, width = rows.shape
    part = width // groups // PLACES
    rows = half(rows).reshape(n, groups, PLACES, part).transpose(2, 0, 1, 3)
    return rows.reshape(PLACES, n, groups * part)


def exchange(pieces):
    return lax.all_to_all(pieces, "tp", split_axis=0, concat_axis=0, tiled=True)


def in_hbm(*arrays):
    return [pltpu.with_memory_space_constraint(v, pltpu.HBM) for v in arrays]


def settings(name, megabytes=40):
    return {
        "compiler_params": pltpu.CompilerParams(vmem_limit_bytes=megabytes << 20),
        "cost_estimate": pl.CostEstimate(flops=1 << 20, bytes_accessed=1 << 20, transcendentals=0),
        "name": name,
    }


def rows_product(lefts, rights, tile, name):
    count, out_rows, out_cols = len(lefts), lefts[0].shape[1], rights[0].shape[1]

    def body(*refs):
        total = None
        for left, right in zip(refs[:count], refs[count : 2 * count], strict=True):
            term = lax.dot_general(
                left[...],
                right[...],
                (((0,), (0,)), ((), ())),
                preferred_element_type=jnp.float32,
            )
            total = term if total is None else total + term
        refs[2 * count][...] = half(total)

    return pl.pallas_call(
        body,
        grid=(out_rows // tile,),
        in_specs=[pl.BlockSpec((v.shape[0], tile), lambda i: (0, i)) for v in lefts]
        + [pl.BlockSpec(v.shape, lambda i: (0, 0)) for v in rights],
        out_specs=pl.BlockSpec((tile, out_cols), lambda i: (i, 0)),
        out_shape=pltpu.HBM((out_rows, out_cols), jnp.bfloat16),
        **settings(name),
    )(*lefts, *rights)


def score_rows(table, keys, queries, heads, query_blocks):
    scores = dot(keys, queries, 1, 1)
    count, key_blocks = queries.shape[0] // BLK, keys.shape[0] // BLK
    lane = lax.broadcasted_iota(jnp.int32, (1, queries.shape[0]), 1)
    down = lax.broadcasted_iota(jnp.int32, (BLK, queries.shape[0]), 0)
    ahead = down - lax.rem(lane, BLK)
    head = table[2 * query_blocks + 2 * key_blocks] + pl.program_id(0)
    slope = jnp.exp2(full(jnp.full(down.shape, head + 1, jnp.int32)) * (-8.0 / heads))
    slant = slope * full(down)
    tiles = []
    for j in range(key_blocks):
        key_pos = table[2 * query_blocks + j]
        key_seg = table[2 * query_blocks + key_blocks + j]
        limit = jnp.zeros((1, queries.shape[0]), jnp.int32)
        for i in range(count):
            block = pl.program_id(1) * count + i
            seen = (key_seg == 0) | (key_seg == table[query_blocks + block])
            here = jnp.where(seen, table[block] - key_pos, -BLK)
            limit = jnp.where(lane >= i * BLK, here, limit)
        tile = scores[j * BLK : (j + 1) * BLK] * (1.0 / math.sqrt(HD))
        tile = tile + (slant + slope * full(key_pos))
        tiles.append(jnp.where(ahead <= limit, tile, NEG_FILL))
    return jnp.concatenate(tiles)


def attend_body(heads, query_blocks, table, query, key, value, attended, level, value_t):
    @pl.when(pl.program_id(1) == 0)
    def turn():
        value_t[...] = half(full(value[...]).T)

    scores = score_rows(table, key[...], query[...], heads, query_blocks)
    top = jnp.max(scores, axis=0, keepdims=True)
    expon = jnp.exp(scores - top)
    total = jnp.sum(expon, axis=0, keepdims=True)
    probs = half(expon * (1.0 / total))
    attended[...] = half(dot(value_t[...], probs, 1, 0).T)
    level[...] = (top + jnp.log(total))[None]


def attend_back_body(
    heads,
    query_blocks,
    my_heads,
    split,
    table,
    query,
    key,
    value,
    level,
    *rest,
):
    rest, grad_parts = rest[len(PARTS) :], rest[: len(PARTS)]
    d_query, d_keys = (rest[0], rest[1]) if split else (rest[0], rest[0])
    grads, key_t, key_acc, value_acc = rest[-4:]
    head, block = pl.program_id(0), pl.program_id(1)
    rows = query.shape[0]
    scale = 1.0 / math.sqrt(HD)

    def columns(place):
        return pl.ds(pl.multiple_of((place * my_heads + head) * HD, HD), HD)

    @pl.when(block == 0)
    def begin():
        begin_row = 0
        for part in grad_parts:
            grads[begin_row : begin_row + part.shape[0], :] = part[...]
            begin_row += part.shape[0]
        key_t[...] = half(full(key[...]).T)
        key_acc[...] = jnp.zeros_like(key_acc)
        value_acc[...] = jnp.zeros_like(value_acc)

    scores = score_rows(table, key[...], query[...], heads, query_blocks)
    probs = jnp.exp(scores - level[0])
    grad = grads[pl.ds(pl.multiple_of(block * rows, rows), rows), :]
    d_probs = dot(value[...], grad, 1, 1)
    delta = jnp.sum(probs * d_probs, axis=0, keepdims=True)
    d_scores = half(probs * (d_probs - delta))
    turned = (dot(key_t[...], d_scores, 1, 0) * scale).T
    d_query[pl.ds(pl.multiple_of(block * rows, rows), rows), columns(0)] = half(turned)
    key_acc[...] += dot(d_scores, query[...], 1, 0)
    value_acc[...] += dot(half(probs), grad, 1, 0)

    @pl.when(block == pl.num_programs(1) - 1)
    def end():
        shift = 0 if split else 1
        d_keys[:, columns(shift)] = half(key_acc[...] * scale)
        d_keys[:, columns(shift + 1)] = half(value_acc[...])


def attention(table, heads, my_heads, query, keys, first, grad=None, level=None):
    rows, total = query.shape[0], keys.shape[0]
    step = 256 if total <= 1024 else BLK
    columns = my_heads * HD
    scalars = pl.BlockSpec(memory_space=pltpu.SMEM)
    of_query = pl.BlockSpec((step, HD), lambda h, i: (i, h))
    of_level = pl.BlockSpec((1, 1, step), lambda h, i: (h, 0, i))
    in_specs = [
        scalars,
        of_query,
        pl.BlockSpec((total, HD), lambda h, i: (0, first + h)),
        pl.BlockSpec((total, HD), lambda h, i: (0, first + my_heads + h)),
    ]
    common = {
        "grid": (my_heads, rows // step),
        "compiler_params": pltpu.CompilerParams(vmem_limit_bytes=48 << 20),
        "cost_estimate": pl.CostEstimate(
            flops=(4 if grad is None else 10) * rows * total * columns,
            bytes_accessed=32 << 20,
            transcendentals=my_heads * rows * total,
        ),
    }
    if grad is None:
        return pl.pallas_call(
            functools.partial(attend_body, heads, rows // BLK),
            in_specs=in_specs,
            out_specs=[of_query, of_level],
            out_shape=[
                jax.ShapeDtypeStruct((rows, columns), jnp.bfloat16),
                jax.ShapeDtypeStruct((my_heads, 1, rows), jnp.float32),
            ],
            scratch_shapes=[pltpu.VMEM((HD, total), jnp.bfloat16)],
            name="attend",
            **common,
        )(table, *in_hbm(query, keys, keys))
    split = query is not keys
    shapes = [(rows, columns), (total, 2 * columns)] if split else [(rows, 3 * columns)]
    return pl.pallas_call(
        functools.partial(attend_back_body, heads, rows // BLK, my_heads, split),
        in_specs=in_specs
        + [of_level]
        + [pl.BlockSpec((part.shape[0], HD), lambda h, i: (0, h)) for part in grad],
        out_specs=[pl.BlockSpec(shape, lambda h, i: (0, 0)) for shape in shapes],
        out_shape=[jax.ShapeDtypeStruct(shape, jnp.bfloat16) for shape in shapes],
        scratch_shapes=[
            pltpu.VMEM((rows, HD), jnp.bfloat16),
            pltpu.VMEM((HD, total), jnp.bfloat16),
            pltpu.VMEM((total, HD), jnp.float32),
            pltpu.VMEM((total, HD), jnp.float32),
        ],
        name="attend_back",
        **common,
    )(table, *in_hbm(query, keys, keys, level, *grad))


def products(parts, matrix, name):
    count, tile = len(parts), 512

    def body(*refs):
        for part, out in zip(refs[:count], refs[count + 1 :], strict=True):
            out[...] = dot(part[...], refs[count][...], 1, 1, jnp.bfloat16)

    return pl.pallas_call(
        body,
        grid=(matrix.shape[0] // tile,),
        in_specs=[pl.BlockSpec(v.shape, lambda i: (0, 0)) for v in parts]
        + [pl.BlockSpec((tile, matrix.shape[1]), lambda i: (i, 0))],
        out_specs=[pl.BlockSpec((v.shape[0], tile), lambda i: (0, i)) for v in parts],
        out_shape=[
            jax.ShapeDtypeStruct((v.shape[0], matrix.shape[0]), jnp.bfloat16) for v in parts
        ],
        **settings(name),
    )(*parts, matrix)


def gather_rows(rows):
    rows = lax.all_gather(rows, TOKENS, axis=1, tiled=True)
    return rows.reshape(-1, rows.shape[2])


def from_places(grad, groups, name):
    places, n, width = grad.shape
    part = width // groups

    def body(grad_ref, out_ref):
        for group in range(groups):
            for place in range(places):
                begin = (group * places + place) * part
                out_ref[:, begin : begin + part] = full(
                    grad_ref[place, :, group * part : (group + 1) * part]
                )

    return pl.pallas_call(
        body,
        out_shape=jax.ShapeDtypeStruct((n, places * width), jnp.float32),
        **settings(name),
    )(grad)


def norm_back(sums, rows, gain, direct, name, branch):
    n, width = rows.shape
    step = 64

    def body(part, upward, downward, rows_ref, gain_ref, direct_ref, grad_ref, *rest):
        @pl.when(pl.program_id(0) == 0)
        def begin():
            for ref in rest[-3 if branch else -2 :]:
                ref[...] = jnp.zeros_like(ref)

        grad = full(part[...]) + full(upward[...]) + full(downward[...])
        normed, scale = normalize(full(rows_ref[...]))
        out = full(direct_ref[...]) + normalize_back(normed, scale, grad * gain_ref[...])
        grad_ref[...] = out
        if branch:
            rounded = half(out)
            rest[0][...] = rounded
            rest[-3][...] += jnp.sum(full(rounded), axis=0, keepdims=True)
        rest[-2][...] += jnp.sum(grad * normed, axis=0, keepdims=True)
        rest[-1][...] += jnp.sum(grad, axis=0, keepdims=True)

    tile = pl.BlockSpec((step, width), lambda i: (i, 0))
    line = pl.BlockSpec((1, width), lambda i: (0, 0))
    lines = 3 if branch else 2
    return pl.pallas_call(
        body,
        grid=(n // step,),
        in_specs=[tile] * 4 + [line, tile],
        out_specs=[tile] * (2 if branch else 1) + [line] * lines,
        out_shape=[jax.ShapeDtypeStruct((n, width), jnp.float32)]
        + [jax.ShapeDtypeStruct((n, width), jnp.bfloat16)] * branch
        + [jax.ShapeDtypeStruct((1, width), jnp.float32)] * lines,
        **settings(name),
    )(*sums, rows, gain.reshape(1, -1), direct)


def converted(values, name):
    def body(values_ref, out_ref):
        out_ref[...] = full(values_ref[...])

    return pl.pallas_call(
        body, out_shape=jax.ShapeDtypeStruct(values.shape, jnp.float32), **settings(name)
    )(values)


def total(sums, rows, bias, name):
    def body(part, upward, downward, rows_ref, bias_ref, out_ref):
        out = full(part[...]) + full(upward[...]) + full(downward[...])
        out_ref[...] = half(rows_ref[...] + out + bias_ref[...])

    return pl.pallas_call(
        body, out_shape=jax.ShapeDtypeStruct(rows.shape, jnp.bfloat16), **settings(name)
    )(*sums, rows, bias.reshape(1, -1))


def rows_by_place(vectors, name):
    widths = [v.shape[1] // PLACES for v in vectors]

    def body(*refs):
        begin = 0
        for ref, width in zip(refs[:-1], widths, strict=True):
            for place in range(PLACES):
                refs[-1][place : place + 1, begin : begin + width] = ref[
                    :, place * width : (place + 1) * width
                ]
            begin += width

    return pl.pallas_call(
        body,
        out_shape=jax.ShapeDtypeStruct((PLACES, sum(widths)), jnp.float32),
        **settings(name),
    )(*vectors)


def with_rows(pieces, rows, name):
    places, n, width = pieces.shape
    more = -(-rows.shape[1] // width)
    padded = -(-more // 8) * 8

    def body(pieces_ref, rows_ref, out_ref):
        out_ref[:, :n, :] = pieces_ref[...]
        out_ref[:, n:, :] = jnp.zeros((places, padded, width), jnp.bfloat16)
        for place in range(places):
            lines = [
                rows_ref[place : place + 1, i * width : (i + 1) * width] for i in range(more)
            ]
            lines.append(jnp.zeros((padded - more, width), jnp.float32))
            out_ref[place, n:, :] = half(jnp.concatenate(lines))

    return pl.pallas_call(
        body,
        out_shape=jax.ShapeDtypeStruct((places, n + padded, width), jnp.bfloat16),
        **settings(name),
    )(pieces, rows)


def from_places_and_rows(received, groups, n, count, name):
    places, padded, width = received.shape
    part = width // groups
    more = count // width

    def body(received_ref, out_ref, sum_ref):
        for group in range(groups):
            for place in range(places):
                begin = (group * places + place) * part
                out_ref[:, begin : begin + part] = full(
                    received_ref[place, :n, group * part : (group + 1) * part]
                )
        lines = jnp.sum(full(received_ref[:, n:, :]), axis=0)
        for i in range(more):
            sum_ref[:, i * width : (i + 1) * width] = lines[i : i + 1]

    return pl.pallas_call(
        body,
        out_shape=[
            jax.ShapeDtypeStruct((n, places * width), jnp.float32),
            jax.ShapeDtypeStruct((1, count), jnp.float32),
        ],
        **settings(name),
    )(received)


def norm_sums(grads, rows, mixed, name):
    width, count, step = rows[0].shape[1], len(rows), 64
    columns = mixed[0].shape[1]

    def body(*refs):
        gain = jnp.zeros((1, width), jnp.float32)
        bias = jnp.zeros((1, width), jnp.float32)
        for grad_ref, rows_ref in zip(refs[:count], refs[count : 2 * count], strict=True):

            def add(i, carried, grad_ref=grad_ref, rows_ref=rows_ref):
                here = pl.ds(pl.multiple_of(i * step, step), step)
                grad = full(grad_ref[here, :])
                normed = normalize(full(rows_ref[here, :]))[0]
                return (
                    carried[0] + jnp.sum(grad * normed, axis=0, keepdims=True),
                    carried[1] + jnp.sum(grad, axis=0, keepdims=True),
                )

            gain, bias = lax.fori_loop(0, rows_ref.shape[0] // step, add, (gain, bias))
        refs[-3][...] = gain
        refs[-2][...] = bias
        refs[-1][...] = sum(
            jnp.sum(full(ref[...]), axis=0, keepdims=True) for ref in refs[2 * count : 3 * count]
        )

    return pl.pallas_call(
        body,
        out_shape=[jax.ShapeDtypeStruct((1, width), jnp.float32)] * 2
        + [jax.ShapeDtypeStruct((1, columns), jnp.float32)],
        **settings(name),
    )(*grads, *rows, *mixed)


def on_device(
    tokens,
    ln1_gain,
    ln1_bias,
    w_qkv,
    b_qv,
    w_out,
    b_out,
    ln2_gain,
    ln2_bias,
    w_in,
    b_in,
    w_down,
    b_down,
    cotangent,
    block_seg,
    block_pos,
):
    sp = lax.axis_size("sp")
    fs = lax.axis_size("fs")
    devices = PLACES * sp * fs
    my_tp = lax.axis_index("tp")
    my_sp = lax.axis_index("sp")
    local_rows, width = tokens.shape[1:]
    heads = width // HD
    my_heads = heads // PLACES
    head_cols = my_heads * HD
    hidden = w_in.shape[1] // PLACES
    group_rows = PLACES * local_rows

    def buffer(columns):
        return jnp.zeros((group_rows, columns), jnp.bfloat16)

    def by_part(rows):
        return [rows[a * local_rows : b * local_rows] for a, b in PARTS]

    order = [[SNAKE[(SNAKE.index(i) + s) % PLACES] for s in SHIFTS] for i in range(PLACES)]
    sources = jnp.asarray(order, jnp.int32)[my_tp]
    picked = (sources[:, None] == jnp.arange(PLACES, dtype=jnp.int32)[None, :]).astype(jnp.int32)

    def in_order(blocks):
        blocks = jnp.sum(picked[:, :, None, None] * blocks.reshape(1, PLACES, sp, -1), axis=1)
        mine = lax.dynamic_index_in_dim(blocks, my_sp, 1, keepdims=False).reshape(-1)
        return mine, blocks.transpose(1, 0, 2).reshape(-1)

    query_seg, key_seg = in_order(block_seg[0])
    query_pos, key_pos = in_order(block_pos[0])
    first_head = jnp.full((1,), my_tp * my_heads, jnp.int32)
    table = jnp.concatenate([query_pos, query_seg, key_pos, key_seg, first_head])

    small = [ln1_gain, ln1_bias, b_out, ln2_gain, ln2_bias, b_down, b_qv, b_in]
    sizes = [v.shape[0] for v in small]
    cuts = [sum(sizes[:i]) for i in range(len(sizes) + 1)]
    own, own_cot = tokens[0], cotangent[0]

    low1, high1 = hop(own, own)
    down_slice = lax.all_gather(half(w_down), TOKENS, axis=0, tiled=True)
    small_own, qkv_pieces = fence(half(jnp.concatenate(small)), by_place(w_qkv, 3))
    qkv_pieces = exchange(qkv_pieces)
    gathered = gather_small(small_own[None], bits_of(EVERY))
    low2, high2 = hop(low1, high1)
    in_pieces = by_place(w_in, 1)
    (
        low1,
        high1,
        low2,
        high2,
        qkv_pieces,
        in_pieces,
        gathered,
        down_slice,
        w_out,
        own_cot,
    ) = fence(
        low1,
        high1,
        low2,
        high2,
        qkv_pieces,
        in_pieces,
        gathered,
        down_slice,
        w_out,
        own_cot,
    )
    gathered = full(gathered)
    gain1, bias1, out_bias, gain2, bias2, down_bias, qv_bias, in_bias = (
        gathered[:, cuts[i] : cuts[i + 1]].reshape(-1) for i in range(len(sizes))
    )
    qv_bias = lax.dynamic_slice_in_dim(qv_bias.reshape(2, width), my_tp * head_cols, head_cols, 1)
    in_bias = lax.dynamic_slice_in_dim(in_bias, my_tp * hidden, hidden)

    def norm1(rows):
        return half(normalize(full(rows))[0] * gain1 + bias1)

    in_pieces = exchange(in_pieces)
    qkv_slice = gather_rows(qkv_pieces)
    out_slice = lax.all_gather(half(w_out), TOKENS, axis=0, tiled=True)
    token_parts = [own, join((low1, high1)), join((low2, high2))]
    low3, high3 = hop(low2, high2)
    normed = [norm1(part) for part in token_parts]
    low3, high3, own_cot, *normed = fence(low3, high3, own_cot, *normed)
    low4, high4 = last_hop(low3, high3)
    token_parts.append(join((low3, high3)))
    normed.append(norm1(token_parts[3]))
    blank = jnp.zeros((head_cols,), jnp.float32)
    qkv_bias = jnp.concatenate([qv_bias[0], blank, qv_bias[1]])
    mixed = [half(dot(part, qkv_slice, 1, 0) + qkv_bias) for part in normed]
    low4, high4, own_cot, qkv_slice, *mixed = fence(low4, high4, own_cot, qkv_slice, *mixed)

    cot_low1, cot_high1 = hop(own_cot, own_cot)
    token_parts.append(join((low4, high4)))
    normed.append(norm1(token_parts[4]))
    mixed = jnp.concatenate([*mixed, half(dot(normed[4], qkv_slice, 1, 0) + qkv_bias)])
    mixed, cot_low1, cot_high1, in_pieces, out_slice = fence(
        mixed, cot_low1, cot_high1, in_pieces, out_slice
    )
    in_slice = lax.all_gather(in_pieces, TOKENS, axis=0, tiled=False)
    in_slice = in_slice.transpose(1, 0, 2, 3).reshape(-1, hidden)
    cot_low2, cot_high2 = hop(cot_low1, cot_high1)
    keys = mixed
    if sp > 1:
        keys = lax.all_gather(mixed[:, head_cols:], "sp", axis=0, tiled=True)
    first_key = my_heads if sp == 1 else 0
    attended, level = attention(table, heads, my_heads, mixed, keys, first_key)
    attended, cot_low2, cot_high2 = fence(attended, cot_low2, cot_high2)

    attended_parts = by_part(attended)
    branch_parts = [dot(attended_parts[i], out_slice, 1, 0, jnp.bfloat16) for i in range(5)]
    branch_low, branch_high = hop(*jnp.split(branch_parts[4], 2))
    cot_low3, cot_high3 = hop(cot_low2, cot_high2)
    branch_low, branch_high, cot_low3, cot_high3, *branch_parts = fence(
        branch_low, branch_high, cot_low3, cot_high3, *branch_parts
    )
    up, down = hop(*first_sum(branch_parts[3], branch_low, branch_high))
    up, down, in_slice = fence(up, down, in_slice)
    up, down = hop(*next_sum(branch_parts[2], up, down))
    cot_parts = [own_cot, join((cot_low1, cot_high1)), join((cot_low2, cot_high2))]
    cot_parts.append(join((cot_low3, cot_high3)))
    up, down, *cot_parts = fence(up, down, *cot_parts)
    up, down = hop(*next_sum(branch_parts[1], up, down))
    up, down, cot_low3, cot_high3 = fence(up, down, cot_low3, cot_high3)
    residual = full(own) + last_sum(branch_parts[0], up, down) + out_bias

    own_normed2, scale2 = normalize(residual)
    second = half(own_normed2 * gain2 + bias2)
    second_parts, act_parts, d_pre_parts, d_second_parts, ffn_parts = [second], [], [], [], []
    low, high = second, second
    for index in range(5):
        if index < 3:
            new_low, new_high = hop(low, high)
        elif index == 3:
            new_low, new_high = last_hop(low, high)
            cot_low4, cot_high4 = last_hop(cot_low3, cot_high3)
        if index:
            second_parts.append(join((low, high)))
        pre_act = dot(second_parts[index], in_slice, 1, 0) + in_bias
        act, gelu_back = jax.vjp(lambda v: jax.nn.gelu(v, approximate=True), pre_act)
        act_parts.append(half(act))
        d_pre = half(gelu_back(dot(cot_parts[index], down_slice, 1, 1))[0])
        d_pre_parts.append(d_pre)
        d_second_parts.append(dot(d_pre, in_slice, 1, 1, jnp.bfloat16))
        made = [act_parts, d_pre_parts, d_second_parts]
        if index < 3:
            ffn_parts.append(dot(act_parts[index], down_slice, 1, 0, jnp.bfloat16))
            made.append(ffn_parts)
        if index < 4:
            low, high, *held = fence(new_low, new_high, *[parts[index] for parts in made])
            for parts, value in zip(made, held, strict=True):
                parts[index] = value
        if index == 3:
            low, cot_low4, cot_high4 = fence(low, cot_low4, cot_high4)
            cot_parts.append(join((cot_low4, cot_high4)))

    low, high = hop(*jnp.split(d_second_parts[4], 2))
    ffn_parts += [dot(act, down_slice, 1, 0, jnp.bfloat16) for act in act_parts[3:]]
    low, high, d_pre_parts[4], act_parts[4], *ffn_parts = fence(
        low, high, d_pre_parts[4], act_parts[4], *ffn_parts
    )
    up, down = hop(*first_sum(d_second_parts[3], low, high))
    out_up, out_down = hop(*jnp.split(ffn_parts[4], 2))
    grad_in = rows_product(second_parts, d_pre_parts, 512, "grad_in")
    grad_in = grad_in.reshape(PLACES, -1, hidden)
    up, down, out_up, out_down, grad_in = fence(up, down, out_up, out_down, grad_in)
    grad_in = lax.psum_scatter(grad_in, TOKENS, scatter_dimension=1, tiled=True)
    up, down = hop(*next_sum(d_second_parts[2], up, down))
    out_up, out_down = hop(*first_sum(ffn_parts[3], out_up, out_down))
    up, down, out_up, out_down, act_parts[4] = fence(up, down, out_up, out_down, act_parts[4])
    up, down = hop(*next_sum(d_second_parts[1], up, down))
    out_up, out_down = next_sum(ffn_parts[2], out_up, out_down)
    grad_down = rows_product(act_parts, cot_parts, 256, "grad_down")
    grad_b_in = sum(jnp.sum(full(part), axis=0) for part in d_pre_parts)
    blank = jnp.zeros((PLACES * hidden,), jnp.float32)
    grad_b_in = lax.dynamic_update_slice_in_dim(blank, grad_b_in, my_tp * hidden, 0)
    g_b_down = jnp.sum(full(own_cot), axis=0)
    up, down, out_up, out_down, grad_down, grad_b_in = fence(
        up, down, out_up, out_down, grad_down, grad_b_in
    )
    grad_down = lax.psum_scatter(grad_down, TOKENS, scatter_dimension=0, tiled=True)

    d_residual, d_branch, g_b_out, g_gain2, g_bias2 = norm_back(
        (d_second_parts[0], up, down), residual, gain2, own_cot, "norm2_back", True
    )
    low, high = hop(d_branch, d_branch)
    low, high = fence(low, high)
    d_branch_parts, d_attended = [d_branch], [dot(d_branch, out_slice, 1, 1, jnp.bfloat16)]
    for index in range(1, 5):
        d_branch_parts.append(join((low, high)))
        d_attended.append(dot(d_branch_parts[index], out_slice, 1, 1, jnp.bfloat16))
        if index < 3:
            low, high = hop(low, high)
            low, high, grad_in, d_attended[index] = fence(low, high, grad_in, d_attended[index])
        elif index == 3:
            low, high = last_hop(low, high)
            low, high, grad_in, d_attended[index], out_up, out_down = fence(
                low, high, grad_in, d_attended[index], out_up, out_down
            )

    out_up, out_down = hop(out_up, out_down)
    grads = attention(table, heads, my_heads, mixed, keys, first_key, d_attended, level)
    if sp == 1:
        (d_mixed,) = grads
    else:
        d_keys = half(lax.psum_scatter(full(grads[1]), "sp", scatter_dimension=0, tiled=True))
        d_mixed = jnp.concatenate([grads[0], d_keys], axis=1)
    d_mixed, d_branch_parts[4], grad_down, out_up, out_down = fence(
        d_mixed, d_branch_parts[4], grad_down, out_up, out_down
    )

    mixed_parts = by_part(d_mixed)
    far = dot(mixed_parts[4], qkv_slice, 1, 1, jnp.bfloat16)
    low, high = hop(*jnp.split(far, 2))
    (near,) = products(mixed_parts[3:4], qkv_slice, "d_normed_near")
    grad_qkv = rows_product(normed, mixed_parts, 512, "grad_qkv")
    grad_qkv = grad_qkv.reshape(PLACES, -1, 3 * head_cols)
    out_up, out_down = hop(*next_sum(ffn_parts[1], out_up, out_down))
    low, high, near, grad_qkv, mixed_parts[0], out_up, out_down = fence(
        low, high, near, grad_qkv, mixed_parts[0], out_up, out_down
    )
    grad_qkv = lax.psum_scatter(grad_qkv, TOKENS, scatter_dimension=1, tiled=True)
    up, down = hop(*first_sum(near, low, high))
    d_normed = [*products(mixed_parts[:3], qkv_slice, "d_normed"), near, far]
    g_gain1, g_bias1, mixed_sum = norm_sums(d_normed, token_parts, mixed_parts, "norm1_sums")
    grad_out = rows_product(attended_parts, d_branch_parts, 128, "grad_out")
    up, down, grad_in, grad_out, g_gain1, g_bias1, mixed_sum, *d_normed[:3] = fence(
        up, down, grad_in, grad_out, g_gain1, g_bias1, mixed_sum, *d_normed[:3]
    )
    up, down = hop(*next_sum(d_normed[2], up, down))
    grad_in = exchange(grad_in)
    grad_b_qv = jnp.zeros((2, width), jnp.float32)
    for i in range(2):
        piece = mixed_sum[:, 2 * i * head_cols : (2 * i + 1) * head_cols]
        grad_b_qv = lax.dynamic_update_slice(grad_b_qv, piece, (i, my_tp * head_cols))
    whole = [g_gain1, g_bias1, g_b_out, g_gain2, g_bias2, g_b_down, grad_b_qv, grad_b_in]
    summed = rows_by_place([v.reshape(1, -1) for v in whole], "sums_by_place")
    summed = sum_small(summed, TOKENS)
    own_rows = grad_qkv.shape[1]
    grad_qkv = with_rows(grad_qkv, summed, "qkv_with_sums")
    up, down, grad_out, grad_in, grad_qkv = fence(up, down, grad_out, grad_in, grad_qkv)
    up, down = hop(*next_sum(d_normed[1], up, down))
    grad_qkv = exchange(grad_qkv)
    grad_w_in = from_places(grad_in, 1, "in_back")
    grad_w_down = converted(grad_down, "down_back")
    output = total((ffn_parts[0], out_up, out_down), residual, down_bias, "output")
    up, down, grad_w_down, grad_w_in, output, grad_qkv = fence(
        up, down, grad_w_down, grad_w_in, output, grad_qkv
    )
    grad_out = lax.psum_scatter(grad_out, TOKENS, scatter_dimension=0, tiled=True)
    grad_tokens = norm_back((d_normed[0], up, down), own, gain1, d_residual, "norm1_back", False)[0]
    grad_w_out = converted(grad_out, "out_back")
    grad_w_qkv, summed = from_places_and_rows(
        grad_qkv, 3, own_rows, summed.shape[1], "qkv_back"
    )
    near_devices = sp * fs
    place = my_sp * fs + lax.axis_index("fs")
    g_gain1, g_bias1, g_b_out, g_gain2, g_bias2, g_b_down, g_b_qv, g_b_in = (
        lax.dynamic_slice_in_dim(summed, cuts[i] * near_devices + place * sizes[i], sizes[i], 1)[0]
        for i in range(len(sizes))
    )
    return (
        output[None],
        grad_tokens[None],
        g_gain1,
        g_bias1,
        grad_w_qkv,
        g_b_qv,
        grad_w_out,
        g_b_out,
        g_gain2,
        g_bias2,
        grad_w_in,
        g_b_in,
        grad_w_down,
        g_b_down,
    )


def solution(mesh):
    ctx, fs = mesh.shape["ctx"], mesh.shape["fsdp"]
    inner = Mesh(mesh.devices.reshape(PLACES, ctx // PLACES, fs), EVERY)
    rows = P("fs", ("tp", "sp"), None)
    vector, matrix, blocks = P(EVERY), P(EVERY, None), P("fs", None)
    kinds = (
        rows,
        vector,
        vector,
        matrix,
        vector,
        matrix,
        vector,
        vector,
        vector,
        matrix,
        vector,
        matrix,
        vector,
    )
    return jax.shard_map(
        on_device,
        mesh=inner,
        in_specs=kinds + (rows, blocks, blocks),
        out_specs=(rows,) + kinds,
        check_vma=False,
    )
```
